32 devices in a mesh: pop: 4 (over y, core), shard: 8 (over z, x).
Axes of the slice: x: 2, y: 2, z: 4, core: 2. Of those that a mesh axis runs over, the one named last changes fastest.
Arguments:
- tokens: bfloat16 [1024, 2048], P('shard'), may hold values from -6 to 6
- targets: bfloat16 [1024, 2048], P('shard'), may hold values from -6 to 6
- norm_gain: float32 [2048], replicated, may hold values from 0.5 to 1.5
- weights: float32 [4, 2, 2048, 256], P('pop', None, 'shard'), may hold values from -6 to 6
- first_moment: float32 [4, 2, 2048, 256], P('pop', None, 'shard'), may hold values from -4 to 4
- second_moment: float32 [4, 2, 2048, 256], P('pop', None, 'shard'), may hold values from 0.05 to 2
- learned_params: float32 [192], replicated, may hold values from -4 to 4
- perturbation: float32 [2, 192], replicated, may hold values from -0.75 to 0.75
- accumulated: float32 [2, 192], replicated, may hold values from -3 to 3
Outputs:
- new_weights: float32 [4, 2, 2048, 256], P('pop', None, 'shard')
- new_first: float32 [4, 2, 2048, 256], P('pop', None, 'shard')
- new_second: float32 [4, 2, 2048, 256], P('pop', None, 'shard')
- unroll_loss: float32 [4], P('pop')
- outer_grad: float32 [192], replicated
The draws below stay inside these ranges and needn't reach their ends.
All inputs are finite; a program needn't handle non-finite values.
Results may differ from the reference program's by a relative error of at most 0.004.
Values may be sent and summed in bfloat16 or wider, within the bound.
A program may use at most 64 MiB of HBM per device.

```python
import math
import jax
import jax.numpy as jnp
from jax import lax

D = 2048
RANK = 256
STEPS = 1
TOK_DEV = 128
LOPT = 192
PARTICLES = 4
PAIRS = 2
TOKENS = 1024
N_SHARD = 8


def steps_of(own_key, shape, shards, least, largest):
    loudness, own = 1.0, jax.random.fold_in(own_key, 6)
    for axis_at, blocks in shards:
        heights = jnp.exp(jax.random.uniform(jax.random.fold_in(own, axis_at), (blocks,), jnp.float32, least / len(shards), largest / len(shards)))
        loudness = loudness * jnp.repeat(heights, shape[axis_at] // blocks).reshape([-1 if axis == axis_at else 1 for axis in range(len(shape))])
    return loudness


def centred(rng, extent, scale, bound, split=(), kind=jnp.bfloat16):
    entries = jax.random.normal(rng, extent, jnp.float32) * scale
    if len(split) > 0:
        entries = steps_of(rng, extent, split, -0.22, 0.18) * entries
    return jnp.clip(entries, min=-bound, max=bound).astype(kind)


def setup_inputs(seed: int = 0) -> dict:
    key_list = jax.random.split(jax.random.key(seed), 10)
    return {
        "tokens": centred(key_list[0], (TOKENS, D), 1.0, 6.0, ((0, 8),)),
        "targets": centred(key_list[1], (TOKENS, D), 1.0, 6.0, ((0, 8),)),
        "norm_gain": jnp.clip(1.0 + 0.1 * jax.random.normal(key_list[2], (D,), jnp.float32), 0.5, 1.5),
        "weights": centred(key_list[3], (PARTICLES, 2, D, RANK), 1.0, 6.0, ((0, 4), (2, 8)), jnp.float32),
        "first_moment": centred(key_list[4], (PARTICLES, 2, D, RANK), 0.3, 4.0, ((0, 4), (2, 8)), jnp.float32),
        "second_moment": jnp.clip(jnp.exp(math.log(2.0) - 3.6888794 * jax.random.uniform(key_list[5], (PARTICLES, 2, D, RANK), jnp.float32) ** steps_of(key_list[5], (PARTICLES, 2, D, RANK), ((0, 4), (2, 8)), -0.2, 0.2)), 0.05, 2.0),
        "learned_params": centred(key_list[6], (LOPT,), 0.5, 4.0, (), jnp.float32),
        "perturbation": centred(key_list[7], (PAIRS, LOPT), 0.05, 0.75, (), jnp.float32),
        "accumulated": centred(key_list[8], (PAIRS, LOPT), 0.2, 3.0, (), jnp.float32),
    }


step_size = 0.1
beta_one = 0.9
beta_two = 0.99
norm_eps = 1e-05
grad_eps = 1e-06

def learned_update(weights, first_state, second_state, gradient, mean_square, learned):
    hidden_units = learned.shape[0] // 6
    scaled = gradient * lax.rsqrt(mean_square + grad_eps)[:, None, None]
    first_new = beta_one * first_state + (1.0 - beta_one) * scaled
    second_new = beta_two * second_state + (1.0 - beta_two) * scaled * scaled
    inverse = lax.rsqrt(second_new)
    momentum = (first_new * inverse).reshape(-1)
    features = jnp.stack([(scaled * inverse).reshape(-1), momentum, weights.reshape(-1)])
    in_map = learned[:3 * hidden_units].reshape(3, hidden_units)
    in_bias = learned[3 * hidden_units:4 * hidden_units]
    out_map = learned[4 * hidden_units:].reshape(2, hidden_units)
    hidden_act = jnp.tanh(jnp.dot(in_map.T, features, precision=lax.Precision.HIGHEST) + in_bias[:, None])
    outputs = jnp.dot(out_map, hidden_act, precision=lax.Precision.HIGHEST)
    change = -step_size * (momentum + outputs[0]) * jnp.exp(jnp.tanh(outputs[1]))
    return (weights + change.reshape(weights.shape), first_new, second_new)

def normalize(tokens, norm_gain):
    values = tokens.astype(jnp.float32)
    inverse = lax.rsqrt(lax.optimization_barrier(jnp.mean(values * values, axis=-1, keepdims=True)) + norm_eps)
    return (values * inverse * norm_gain).astype(jnp.bfloat16)

def block_sum(normed_blocks, right_blocks, factor):
    parts = jnp.einsum('jtd,jtr->jdr', normed_blocks.astype(jnp.float32), right_blocks.astype(jnp.float32)) * factor
    rounded = lax.optimization_barrier(parts.astype(jnp.bfloat16))
    return lax.optimization_barrier(jnp.sum(rounded.astype(jnp.float32), axis=0))

def reference(tokens, targets, norm_gain, weights, first_moment, second_moment, learned_params, perturbation, accumulated):
    normed = normalize(tokens, norm_gain)
    tokens_wide = tokens.astype(jnp.float32)
    target_wide = targets.astype(jnp.float32)
    down_scale = D ** (-0.5)
    up_scale = RANK ** (-0.5)

    def particle(inputs):
        particle_index, current, first_state, second_state = inputs
        polarity = (1 - 2 * (particle_index % 2)).astype(jnp.float32)
        learned = learned_params + polarity * perturbation[particle_index // 2]
        running_loss = jnp.zeros((), jnp.float32)
        for unroll_step in range(STEPS):
            rounded = current.astype(jnp.bfloat16)
            branch_input = jnp.dot(normed, rounded[0], preferred_element_type=jnp.float32) * down_scale
            active = jax.nn.silu(branch_input).astype(jnp.bfloat16)
            branch = lax.dot_general(active, rounded[1], (((1,), (1,)), ((), ())), preferred_element_type=jnp.float32) * up_scale
            residual = tokens_wide + branch - target_wide
            running_loss = running_loss + jnp.sum(residual * residual) / (TOKENS * D)
            upstream = (2.0 * residual).astype(jnp.bfloat16)
            back_act = jnp.dot(upstream, rounded[1], preferred_element_type=jnp.float32) * up_scale
            logistic = jax.nn.sigmoid(branch_input)
            back = (back_act * logistic * (1.0 + branch_input * (1.0 - logistic))).astype(jnp.bfloat16)
            grad_down = block_sum(normed.reshape(N_SHARD, TOK_DEV, D), back.reshape(N_SHARD, TOK_DEV, RANK), down_scale)
            grad_up = block_sum(upstream.reshape(N_SHARD, TOK_DEV, D), active.reshape(N_SHARD, TOK_DEV, RANK), up_scale)
            gradient = jnp.stack([grad_down, grad_up])
            mean_square = lax.optimization_barrier(jnp.mean(gradient * gradient, axis=(1, 2)))
            current, first_state, second_state = learned_update(current, first_state, second_state, gradient, mean_square, learned)
        return (current, first_state, second_state, running_loss)
    indices = jnp.arange(PARTICLES, dtype=jnp.int32)
    new_weights, new_first, new_second, unroll_loss = lax.map(particle, (indices, weights, first_moment, second_moment))
    pair_diff = unroll_loss[0::2] - unroll_loss[1::2]
    outer_grad = jnp.dot(pair_diff, accumulated + perturbation, precision=lax.Precision.HIGHEST) / (2 * PAIRS)
    return (new_weights, new_first, new_second, unroll_loss, outer_grad)
```

```python
import functools
import math

import jax
import jax.numpy as jnp
from jax import lax
from jax.experimental import pallas as pl
from jax.experimental.pallas import tpu as pltpu
from jax.sharding import PartitionSpec as P

step_size = 0.1
beta_one = 0.9
beta_two = 0.99
norm_eps = 1e-05
grad_eps = 1e-06

LANES = 128
MESH = pl.DeviceIdType.MESH


def grid_of(n):
    nx = max(1, math.isqrt(n // 2))
    while n % nx:
        nx -= 1
    return n // nx, nx


def shard_at(pos, nz, nx):
    x = pos // nz
    zz = pos % nz
    z = zz + (x % 2) * (nz - 1 - 2 * zz)
    return z * nx + x


def position_of(shard, nz, nx):
    x = shard % nx
    z = shard // nx
    zz = z + (x % 2) * (nz - 1 - 2 * z)
    return x * nz + zz


class Ring:
    def __init__(self, n, block, sends, recvs, far):
        self.n, self.block, self.sends, self.recvs = n, block, sends, recvs
        self.nz, self.nx = grid_of(n)
        self.pos = position_of(lax.axis_index("shard"), self.nz, self.nx)
        half = n // 2
        self.hops = (half, n - 1 - half) if far == 0 else (n - 1 - half, half)

    def shard(self, pos):
        return shard_at(lax.rem(pos + 2 * self.n, self.n), self.nz, self.nx)

    def copy(self, way, hop, arriving=False):
        sign = 1 if way == 0 else -1
        back = hop + 1 if arriving else hop
        ref = self.block(self.shard(self.pos - sign * back))
        at = way * (self.n // 2 + 1) + hop
        return pltpu.make_async_remote_copy(
            src_ref=ref,
            dst_ref=ref,
            send_sem=self.sends.at[at],
            recv_sem=self.recvs.at[at],
            device_id={"shard": self.shard(self.pos + sign)},
            device_id_type=MESH,
        )

    def step(self, hop):
        for way in (0, 1):
            if 1 <= hop <= self.hops[way]:
                self.copy(way, hop - 1, arriving=True).wait_recv()
            if hop < self.hops[way]:
                self.copy(way, hop).start()

    def drain(self):
        for way in (0, 1):
            for hop in range(self.hops[way]):
                self.copy(way, hop).wait_send()


class Direct:
    def __init__(self, axis, n, source, slot, sends, recvs):
        self.axis, self.n, self.source, self.slot = axis, n, source, slot
        self.sends, self.recvs = sends, recvs
        self.me = lax.axis_index(axis)

    def copy(self, off, arriving=False):
        to = lax.rem(self.me + off, self.n)
        owner = lax.rem(self.me + self.n - off, self.n) if arriving else self.me
        return pltpu.make_async_remote_copy(
            src_ref=self.source(to),
            dst_ref=self.slot(owner),
            send_sem=self.sends.at[off - 1],
            recv_sem=self.recvs.at[off - 1],
            device_id={self.axis: to},
            device_id_type=MESH,
        )

    def start(self):
        for off in range(1, self.n):
            self.copy(off).start()

    def wait_recv(self):
        for off in range(1, self.n):
            self.copy(off, arriving=True).wait_recv()

    def drain(self):
        for off in range(1, self.n):
            self.copy(off).wait_send()


def total_of(values):
    return jnp.sum(jnp.sum(values, axis=0, keepdims=True), axis=1, keepdims=True)


def exchange_kernel(
    n,
    npop,
    tokens_ref,
    targets_ref,
    gain_ref,
    weights_ref,
    grad_ref,
    stats_ref,
    losses_ref,
    gathered,
    normed,
    normed_t,
    upstream_t,
    normed_in,
    upstream_in,
    active_all,
    back_all,
    loss_own,
    loss_in,
    square_own,
    square_in,
    pop_own,
    pop_in,
    ring_send,
    ring_recv,
    direct_send,
    direct_recv,
    pop_send,
    pop_recv,
):
    me = lax.axis_index("shard")
    mine = lax.axis_index("pop")
    width = tokens_ref.shape[1]
    rows = width // n
    token_rows = tokens_ref.shape[0]
    rank = weights_ref.shape[-1]
    down_scale = width ** (-0.5)
    up_scale = rank ** (-0.5)

    barrier = pltpu.get_barrier_semaphore()
    for off in range(1, n):
        pl.semaphore_signal(
            barrier, inc=1, device_id={"shard": lax.rem(me + off, n)}, device_id_type=MESH
        )
    for off in range(1, npop):
        pl.semaphore_signal(
            barrier, inc=1, device_id={"pop": lax.rem(mine + off, npop)}, device_id_type=MESH
        )

    def row_block(index):
        return pl.ds(pl.multiple_of(index * rows, rows), rows)

    for part in (0, 1):
        gathered[part, row_block(me), :] = weights_ref[0, part].astype(jnp.bfloat16)
    pl.semaphore_wait(barrier, n - 1 + npop - 1)

    rings = [
        Ring(n, block, ring_send.at[i], ring_recv.at[i], far)
        for i, (block, far) in enumerate(
            [
                (lambda s: gathered.at[0, row_block(s), :], 0),
                (lambda s: gathered.at[1, row_block(s), :], 1),
                (lambda s: active_all.at[s], 0),
                (lambda s: back_all.at[s], 1),
            ]
        )
    ]
    down_ring, up_ring, active_ring, back_ring = rings
    normed_out = Direct(
        "shard", n, lambda s: normed_t.at[row_block(s), :], lambda s: normed_in.at[s],
        direct_send.at[0], direct_recv.at[0],
    )
    upstream_out = Direct(
        "shard", n, lambda s: upstream_t.at[row_block(s), :], lambda s: upstream_in.at[s],
        direct_send.at[1], direct_recv.at[1],
    )
    loss_out = Direct(
        "shard", n, lambda s: loss_own, lambda s: loss_in.at[s],
        direct_send.at[2], direct_recv.at[2],
    )
    square_out = Direct(
        "shard", n, lambda s: square_own, lambda s: square_in.at[s],
        direct_send.at[3], direct_recv.at[3],
    )
    pop_out = Direct(
        "pop", npop, lambda s: pop_own, lambda s: pop_in.at[s], pop_send, pop_recv
    )

    down_ring.step(0)
    up_ring.step(0)

    chunk = 256
    squares = jnp.zeros((token_rows, LANES), jnp.float32)
    for at in range(0, width, LANES):
        values = tokens_ref[:, at : at + LANES].astype(jnp.float32)
        squares += values * values
    mean = jnp.sum(squares, axis=1, keepdims=True) / width
    inverse = lax.rsqrt(mean + norm_eps)
    for at in range(0, width, LANES):
        values = tokens_ref[:, at : at + LANES].astype(jnp.float32)
        values = values * inverse * gain_ref[:, at : at + LANES]
        normed[:, at : at + LANES] = values.astype(jnp.bfloat16)
        normed_t[at : at + LANES, :] = values.T.astype(jnp.bfloat16)
    normed_in[me] = normed_t[row_block(me), :]

    last = n // 2
    for hop in range(1, last):
        down_ring.step(hop)
        up_ring.step(hop)
    down_ring.step(last)
    normed_out.start()

    pre = jnp.zeros((token_rows, rank), jnp.float32)
    for at in range(0, width, chunk):
        pre += jnp.dot(
            normed[:, at : at + chunk],
            gathered[0, at : at + chunk, :],
            preferred_element_type=jnp.float32,
        )
    pre = pre * down_scale
    logistic = jax.nn.sigmoid(pre)
    active = (pre * logistic).astype(jnp.bfloat16)
    active_all[me] = active
    active_ring.step(0)
    slope = logistic * (1.0 + pre * (1.0 - logistic)) * up_scale
    up_ring.step(last)

    loss = jnp.zeros((1, 1), jnp.float32)
    back = jnp.zeros((token_rows, rank), jnp.float32)
    for at in range(0, width, chunk):
        held = gathered[1, at : at + chunk, :]
        branch = lax.dot_general(
            active, held, (((1,), (1,)), ((), ())), preferred_element_type=jnp.float32
        )
        residual = (
            tokens_ref[:, at : at + chunk].astype(jnp.float32)
            + branch * up_scale
            - targets_ref[:, at : at + chunk].astype(jnp.float32)
        )
        loss += total_of(residual * residual)
        double = 2.0 * residual
        back += jnp.dot(double.astype(jnp.bfloat16), held, preferred_element_type=jnp.float32)
        for sub in range(0, chunk, LANES):
            upstream_t[at + sub : at + sub + LANES, :] = double[:, sub : sub + LANES].T.astype(
                jnp.bfloat16
            )
    back_all[me] = (back * slope).astype(jnp.bfloat16)
    loss_own[...] = jnp.broadcast_to(loss, loss_own.shape)
    back_ring.step(0)
    active_ring.step(1)
    upstream_out.start()
    loss_out.start()
    upstream_in[me] = upstream_t[row_block(me), :]
    loss_in[me] = loss_own[...]
    for hop in range(1, last + 1):
        back_ring.step(hop)
        if hop > 1:
            active_ring.step(hop)
    normed_out.wait_recv()

    total = jnp.zeros((1, 1), jnp.float32)
    sums = []
    for part in (0, 1):
        left, right = ((normed_in, back_all), (upstream_in, active_all))[part]
        if part == 1:
            upstream_out.wait_recv()
        acc = jnp.zeros((rows, rank), jnp.float32)
        for j in range(n):
            acc += jnp.dot(left[j], right[j], preferred_element_type=jnp.float32)
        acc = acc * (down_scale, up_scale)[part]
        grad_ref[part] = acc
        sums.append(total_of(acc * acc))
    sub = lax.broadcasted_iota(jnp.int32, square_own.shape, 0)
    square_own[...] = jnp.where(
        sub == 0,
        jnp.broadcast_to(sums[0], square_own.shape),
        jnp.broadcast_to(sums[1], square_own.shape),
    )
    square_out.start()
    square_in[me] = square_own[...]
    loss_out.wait_recv()
    group = loss_in[0]
    for j in range(1, n):
        group += loss_in[j]
    pop_own[...] = group
    pop_out.start()
    pop_in[mine] = group
    square_out.wait_recv()
    both = square_in[0]
    for j in range(1, n):
        both += square_in[j]
    stats_ref[...] = both
    pop_out.wait_recv()
    losses_ref[...] = pop_in[...]
    for item in (*rings, normed_out, upstream_out, loss_out, square_out, pop_out):
        item.drain()


def exchange(mesh_shape, tokens, targets, gain, weights):
    n, npop = mesh_shape["shard"], mesh_shape["pop"]
    token_rows, width = tokens.shape
    rank = weights.shape[-1]
    rows = width // n
    wide, narrow = jnp.float32, jnp.bfloat16
    tile = (8, LANES)
    vmem = pl.BlockSpec(memory_space=pltpu.VMEM)
    return pl.pallas_call(
        functools.partial(exchange_kernel, n, npop),
        out_shape=(
            jax.ShapeDtypeStruct((2, rows, rank), wide),
            jax.ShapeDtypeStruct(tile, wide),
            jax.ShapeDtypeStruct((npop, *tile), wide),
        ),
        in_specs=[vmem] * 4,
        out_specs=(vmem, vmem, vmem),
        scratch_shapes=[
            pltpu.VMEM((2, width, rank), narrow),
            pltpu.VMEM((token_rows, width), narrow),
            pltpu.VMEM((width, token_rows), narrow),
            pltpu.VMEM((width, token_rows), narrow),
            pltpu.VMEM((n, rows, token_rows), narrow),
            pltpu.VMEM((n, rows, token_rows), narrow),
            pltpu.VMEM((n, token_rows, rank), narrow),
            pltpu.VMEM((n, token_rows, rank), narrow),
            pltpu.VMEM(tile, wide),
            pltpu.VMEM((n, *tile), wide),
            pltpu.VMEM(tile, wide),
            pltpu.VMEM((n, *tile), wide),
            pltpu.VMEM(tile, wide),
            pltpu.VMEM((npop, *tile), wide),
            pltpu.SemaphoreType.DMA((4, n + 2)),
            pltpu.SemaphoreType.DMA((4, n + 2)),
            pltpu.SemaphoreType.DMA((4, n)),
            pltpu.SemaphoreType.DMA((4, n)),
            pltpu.SemaphoreType.DMA((npop,)),
            pltpu.SemaphoreType.DMA((npop,)),
        ],
        compiler_params=pltpu.CompilerParams(
            collective_id=0, has_side_effects=True, vmem_limit_bytes=40 << 20
        ),
        name="exchange",
    )(tokens, targets, gain, weights)


def update_kernel(
    count, units, learned_ref, stats_ref, grad_ref, weights_ref, first_ref, second_ref,
    weights_out, first_out, second_out,
):
    part = pl.program_id(0)
    height = grad_ref.shape[1]
    block = min(32, height)
    square = jnp.where(part == 0, stats_ref[0:1, 0:1], stats_ref[1:2, 0:1])
    scale = lax.rsqrt(square / count + grad_eps)

    @pl.loop(0, height // block)
    def _(at):
        here = pl.ds(pl.multiple_of(at * block, block), block)
        scaled = grad_ref[0, here, :] * scale
        first = beta_one * first_ref[0, 0, here, :] + (1.0 - beta_one) * scaled
        second = beta_two * second_ref[0, 0, here, :] + (1.0 - beta_two) * scaled * scaled
        first_out[0, 0, here, :] = first
        second_out[0, 0, here, :] = second
        inverse = lax.rsqrt(second)
        slope = scaled * inverse
        momentum = first * inverse
        held = weights_ref[0, 0, here, :]
        shift = momentum
        gate = jnp.zeros_like(momentum)
        for unit in range(units):
            hidden = jnp.tanh(
                slope * learned_ref[unit]
                + momentum * learned_ref[units + unit]
                + (held * learned_ref[2 * units + unit] + learned_ref[3 * units + unit])
            )
            shift = shift + hidden * learned_ref[4 * units + unit]
            gate = gate + hidden * learned_ref[5 * units + unit]
        weights_out[0, 0, here, :] = held - step_size * shift * jnp.exp(jnp.tanh(gate))


def update(learned, stats, grad, weights, first, second, count):
    _, _, rows, rank = weights.shape
    height = min(rows, 128)
    spec = pl.BlockSpec((1, 1, height, rank), lambda p, i: (0, p, i, 0))
    shape = jax.ShapeDtypeStruct(weights.shape, jnp.float32)
    return pl.pallas_call(
        functools.partial(update_kernel, count, learned.shape[0] // 6),
        grid=(2, rows // height),
        out_shape=(shape, shape, shape),
        in_specs=[
            pl.BlockSpec(memory_space=pltpu.SMEM),
            pl.BlockSpec((8, LANES), lambda p, i: (0, 0)),
            pl.BlockSpec((1, height, rank), lambda p, i: (p, i, 0)),
            spec,
            spec,
            spec,
        ],
        out_specs=(spec, spec, spec),
        name="update",
    )(learned, stats, grad, weights, first, second)


def local(
    mesh_shape,
    tokens,
    targets,
    norm_gain,
    weights,
    first_moment,
    second_moment,
    learned_params,
    perturbation,
    accumulated,
):
    n, npop = mesh_shape["shard"], mesh_shape["pop"]
    token_rows, width = tokens.shape
    rank = weights.shape[-1]
    pop_index = lax.axis_index("pop")
    polarity = (1 - 2 * (pop_index % 2)).astype(jnp.float32)
    learned = learned_params + polarity * lax.dynamic_index_in_dim(
        perturbation, pop_index // 2, 0, keepdims=False
    )
    grad, stats, losses = exchange(mesh_shape, tokens, targets, norm_gain[None], weights)
    new_weights, new_first, new_second = update(
        learned, stats, grad, weights, first_moment, second_moment, width * rank
    )
    per_particle = losses[:, 0, 0] / (token_rows * n * width)
    unroll = lax.dynamic_slice_in_dim(per_particle, pop_index, 1)
    differ = per_particle[0::2] - per_particle[1::2]
    outer = jnp.sum(differ[:, None] * (accumulated + perturbation), axis=0) / (2 * (npop // 2))
    return (new_weights, new_first, new_second, unroll, outer)


def solution(mesh):
    rows = P("pop", None, "shard", None)
    return jax.shard_map(
        functools.partial(local, dict(mesh.shape)),
        mesh=mesh,
        in_specs=(P("shard", None), P("shard", None), P(), rows, rows, rows, P(), P(), P()),
        out_specs=(rows, rows, rows, P("pop"), P()),
        check_vma=False,
    )
```

```python
import functools
import math

import jax
import jax.numpy as jnp
from jax import lax
from jax.experimental import pallas as pl
from jax.experimental.pallas import tpu as pltpu
from jax.sharding import PartitionSpec as P

step_size = 0.1
beta_one = 0.9
beta_two = 0.99
norm_eps = 1e-05
grad_eps = 1e-06

LANES = 128
MESH = pl.DeviceIdType.MESH


def grid_of(n):
    nx = max(1, math.isqrt(n // 2))
    while n % nx:
        nx -= 1
    return n // nx, nx


def shard_at(pos, nz, nx):
    x = pos // nz
    zz = pos % nz
    z = zz + (x % 2) * (nz - 1 - 2 * zz)
    return z * nx + x


def position_of(shard, nz, nx):
    x = shard % nx
    z = shard // nx
    zz = z + (x % 2) * (nz - 1 - 2 * z)
    return x * nz + zz


class Ring:
    def __init__(self, n, block, sends, recvs, far):
        self.n, self.block, self.sends, self.recvs = n, block, sends, recvs
        self.nz, self.nx = grid_of(n)
        self.pos = position_of(lax.axis_index("shard"), self.nz, self.nx)
        half = n // 2
        self.hops = (half, n - 1 - half) if far == 0 else (n - 1 - half, half)

    def shard(self, pos):
        return shard_at(lax.rem(pos + 2 * self.n, self.n), self.nz, self.nx)

    def copy(self, way, hop, arriving=False):
        sign = 1 if way == 0 else -1
        back = hop + 1 if arriving else hop
        ref = self.block(self.shard(self.pos - sign * back))
        at = way * (self.n // 2 + 1) + hop
        return pltpu.make_async_remote_copy(
            src_ref=ref,
            dst_ref=ref,
            send_sem=self.sends.at[at],
            recv_sem=self.recvs.at[at],
            device_id={"shard": self.shard(self.pos + sign)},
            device_id_type=MESH,
        )

    def step(self, hop):
        for way in (0, 1):
            if 1 <= hop <= self.hops[way]:
                self.copy(way, hop - 1, arriving=True).wait_recv()
            if hop < self.hops[way]:
                self.copy(way, hop).start()

    def drain(self):
        for way in (0, 1):
            for hop in range(self.hops[way]):
                self.copy(way, hop).wait_send()


class Direct:
    def __init__(self, axis, n, source, slot, sends, recvs):
        self.axis, self.n, self.source, self.slot = axis, n, source, slot
        self.sends, self.recvs = sends, recvs
        self.me = lax.axis_index(axis)

    def copy(self, off, arriving=False):
        to = lax.rem(self.me + off, self.n)
        owner = lax.rem(self.me + self.n - off, self.n) if arriving else self.me
        return pltpu.make_async_remote_copy(
            src_ref=self.source(to),
            dst_ref=self.slot(owner),
            send_sem=self.sends.at[off - 1],
            recv_sem=self.recvs.at[off - 1],
            device_id={self.axis: to},
            device_id_type=MESH,
        )

    def start(self):
        for off in range(1, self.n):
            self.copy(off).start()

    def wait_recv(self):
        for off in range(1, self.n):
            self.copy(off, arriving=True).wait_recv()

    def drain(self):
        for off in range(1, self.n):
            self.copy(off).wait_send()


def total_of(values):
    return jnp.sum(jnp.sum(values, axis=0, keepdims=True), axis=1, keepdims=True)


def exchange_kernel(
    n,
    npop,
    tokens_hbm,
    targets_hbm,
    gain_hbm,
    weights_hbm,
    grad_ref,
    stats_ref,
    losses_ref,
    tokens_ref,
    targets_ref,
    gain_ref,
    weights_ref,
    load_sem,
    gathered,
    normed,
    normed_t,
    upstream_t,
    normed_in,
    upstream_in,
    active_all,
    back_all,
    loss_own,
    loss_in,
    square_own,
    square_in,
    pop_own,
    pop_in,
    ring_send,
    ring_recv,
    direct_send,
    direct_recv,
    pop_send,
    pop_recv,
):
    me = lax.axis_index("shard")
    mine = lax.axis_index("pop")
    width = tokens_ref.shape[1]
    rows = width // n
    token_rows = tokens_ref.shape[0]
    rank = weights_ref.shape[-1]
    down_scale = width ** (-0.5)
    up_scale = rank ** (-0.5)

    loads = [
        pltpu.make_async_copy(source, target, load_sem.at[i])
        for i, (source, target) in enumerate(
            [
                (weights_hbm, weights_ref),
                (tokens_hbm, tokens_ref),
                (gain_hbm, gain_ref),
                (targets_hbm, targets_ref),
            ]
        )
    ]
    barrier = pltpu.get_barrier_semaphore()
    for load in loads:
        load.start()
    for off in range(1, n):
        pl.semaphore_signal(
            barrier, inc=1, device_id={"shard": lax.rem(me + off, n)}, device_id_type=MESH
        )
    for off in range(1, npop):
        pl.semaphore_signal(
            barrier, inc=1, device_id={"pop": lax.rem(mine + off, npop)}, device_id_type=MESH
        )

    def row_block(index):
        return pl.ds(pl.multiple_of(index * rows, rows), rows)

    loads[0].wait()
    for part in (0, 1):
        gathered[part, row_block(me), :] = weights_ref[0, part].astype(jnp.bfloat16)
    pl.semaphore_wait(barrier, n - 1 + npop - 1)

    rings = [
        Ring(n, block, ring_send.at[i], ring_recv.at[i], far)
        for i, (block, far) in enumerate(
            [
                (lambda s: gathered.at[0, row_block(s), :], 0),
                (lambda s: gathered.at[1, row_block(s), :], 1),
                (lambda s: active_all.at[s], 0),
                (lambda s: back_all.at[s], 1),
            ]
        )
    ]
    down_ring, up_ring, active_ring, back_ring = rings
    normed_out = Direct(
        "shard", n, lambda s: normed_t.at[row_block(s), :], lambda s: normed_in.at[s],
        direct_send.at[0], direct_recv.at[0],
    )
    upstream_out = Direct(
        "shard", n, lambda s: upstream_t.at[row_block(s), :], lambda s: upstream_in.at[s],
        direct_send.at[1], direct_recv.at[1],
    )
    loss_out = Direct(
        "shard", n, lambda s: loss_own, lambda s: loss_in.at[s],
        direct_send.at[2], direct_recv.at[2],
    )
    square_out = Direct(
        "shard", n, lambda s: square_own, lambda s: square_in.at[s],
        direct_send.at[3], direct_recv.at[3],
    )
    pop_out = Direct(
        "pop", npop, lambda s: pop_own, lambda s: pop_in.at[s], pop_send, pop_recv
    )

    down_ring.step(0)
    up_ring.step(0)

    loads[1].wait()
    loads[2].wait()
    chunk = 256
    squares = jnp.zeros((token_rows, LANES), jnp.float32)
    for at in range(0, width, LANES):
        values = tokens_ref[:, at : at + LANES].astype(jnp.float32)
        squares += values * values
    mean = jnp.sum(squares, axis=1, keepdims=True) / width
    inverse = lax.rsqrt(mean + norm_eps)
    for at in range(0, width, LANES):
        values = tokens_ref[:, at : at + LANES].astype(jnp.float32)
        values = values * inverse * gain_ref[:, at : at + LANES]
        normed[:, at : at + LANES] = values.astype(jnp.bfloat16)
        normed_t[at : at + LANES, :] = values.T.astype(jnp.bfloat16)
    normed_in[me] = normed_t[row_block(me), :]

    last = n // 2
    for hop in range(1, last):
        down_ring.step(hop)
        up_ring.step(hop)
    down_ring.step(last)
    normed_out.start()

    pre = jnp.zeros((token_rows, rank), jnp.float32)
    for at in range(0, width, chunk):
        pre += jnp.dot(
            normed[:, at : at + chunk],
            gathered[0, at : at + chunk, :],
            preferred_element_type=jnp.float32,
        )
    pre = pre * down_scale
    logistic = jax.nn.sigmoid(pre)
    active = (pre * logistic).astype(jnp.bfloat16)
    active_all[me] = active
    active_ring.step(0)
    slope = logistic * (1.0 + pre * (1.0 - logistic)) * up_scale
    up_ring.step(last)

    loads[3].wait()
    loss = jnp.zeros((1, 1), jnp.float32)
    back = jnp.zeros((token_rows, rank), jnp.float32)
    for at in range(0, width, chunk):
        held = gathered[1, at : at + chunk, :]
        branch = lax.dot_general(
            active, held, (((1,), (1,)), ((), ())), preferred_element_type=jnp.float32
        )
        residual = (
            tokens_ref[:, at : at + chunk].astype(jnp.float32)
            + branch * up_scale
            - targets_ref[:, at : at + chunk].astype(jnp.float32)
        )
        loss += total_of(residual * residual)
        double = 2.0 * residual
        back += jnp.dot(double.astype(jnp.bfloat16), held, preferred_element_type=jnp.float32)
        for sub in range(0, chunk, LANES):
            upstream_t[at + sub : at + sub + LANES, :] = double[:, sub : sub + LANES].T.astype(
                jnp.bfloat16
            )
    back_all[me] = (back * slope).astype(jnp.bfloat16)
    loss_own[...] = jnp.broadcast_to(loss, loss_own.shape)
    back_ring.step(0)
    active_ring.step(1)
    upstream_out.start()
    loss_out.start()
    upstream_in[me] = upstream_t[row_block(me), :]
    loss_in[me] = loss_own[...]
    for hop in range(1, last + 1):
        back_ring.step(hop)
        if hop > 1:
            active_ring.step(hop)
    normed_out.wait_recv()

    total = jnp.zeros((1, 1), jnp.float32)
    sums = []
    for part in (0, 1):
        left, right = ((normed_in, back_all), (upstream_in, active_all))[part]
        if part == 1:
            upstream_out.wait_recv()
        acc = jnp.zeros((rows, rank), jnp.float32)
        for j in range(n):
            acc += jnp.dot(left[j], right[j], preferred_element_type=jnp.float32)
        acc = acc * (down_scale, up_scale)[part]
        grad_ref[part] = acc
        sums.append(total_of(acc * acc))
    sub = lax.broadcasted_iota(jnp.int32, square_own.shape, 0)
    square_own[...] = jnp.where(
        sub == 0,
        jnp.broadcast_to(sums[0], square_own.shape),
        jnp.broadcast_to(sums[1], square_own.shape),
    )
    square_out.start()
    square_in[me] = square_own[...]
    loss_out.wait_recv()
    group = loss_in[0]
    for j in range(1, n):
        group += loss_in[j]
    pop_own[...] = group
    pop_out.start()
    pop_in[mine] = group
    square_out.wait_recv()
    both = square_in[0]
    for j in range(1, n):
        both += square_in[j]
    stats_ref[...] = both
    pop_out.wait_recv()
    losses_ref[...] = pop_in[...]
    for item in (*rings, normed_out, upstream_out, loss_out, square_out, pop_out):
        item.drain()


def exchange(mesh_shape, tokens, targets, gain, weights):
    n, npop = mesh_shape["shard"], mesh_shape["pop"]
    token_rows, width = tokens.shape
    rank = weights.shape[-1]
    rows = width // n
    wide, narrow = jnp.float32, jnp.bfloat16
    tile = (8, LANES)
    vmem = pl.BlockSpec(memory_space=pltpu.VMEM)
    anywhere = pl.BlockSpec(memory_space=pl.ANY)
    return pl.pallas_call(
        functools.partial(exchange_kernel, n, npop),
        out_shape=(
            jax.ShapeDtypeStruct((2, rows, rank), wide),
            jax.ShapeDtypeStruct(tile, wide),
            jax.ShapeDtypeStruct((npop, *tile), wide),
        ),
        in_specs=[anywhere] * 4,
        out_specs=(vmem, vmem, vmem),
        scratch_shapes=[
            pltpu.VMEM(tokens.shape, tokens.dtype),
            pltpu.VMEM(targets.shape, targets.dtype),
            pltpu.VMEM(gain.shape, gain.dtype),
            pltpu.VMEM(weights.shape, weights.dtype),
            pltpu.SemaphoreType.DMA((4,)),
            pltpu.VMEM((2, width, rank), narrow),
            pltpu.VMEM((token_rows, width), narrow),
            pltpu.VMEM((width, token_rows), narrow),
            pltpu.VMEM((width, token_rows), narrow),
            pltpu.VMEM((n, rows, token_rows), narrow),
            pltpu.VMEM((n, rows, token_rows), narrow),
            pltpu.VMEM((n, token_rows, rank), narrow),
            pltpu.VMEM((n, token_rows, rank), narrow),
            pltpu.VMEM(tile, wide),
            pltpu.VMEM((n, *tile), wide),
            pltpu.VMEM(tile, wide),
            pltpu.VMEM((n, *tile), wide),
            pltpu.VMEM(tile, wide),
            pltpu.VMEM((npop, *tile), wide),
            pltpu.SemaphoreType.DMA((4, n + 2)),
            pltpu.SemaphoreType.DMA((4, n + 2)),
            pltpu.SemaphoreType.DMA((4, n)),
            pltpu.SemaphoreType.DMA((4, n)),
            pltpu.SemaphoreType.DMA((npop,)),
            pltpu.SemaphoreType.DMA((npop,)),
        ],
        compiler_params=pltpu.CompilerParams(
            collective_id=0, has_side_effects=True
        ),
        name="exchange",
    )(tokens, targets, gain, weights)


def update_kernel(
    npop, count, loss_count, base_ref, shift_ref, stats_ref, losses_ref, perturbation_ref,
    accumulated_ref, grad_ref, weights_ref, first_ref, second_ref,
    weights_out, first_out, second_out, unroll_out, outer_out, learned_ref,
):
    part = pl.program_id(0)
    mine = lax.axis_index("pop")
    units = base_ref.shape[0] // 6
    height = grad_ref.shape[1]
    block = min(32, height)

    @pl.when((part == 0) & (pl.program_id(1) == 0))
    def _():
        polarity = (1 - 2 * lax.rem(mine, 2)).astype(jnp.float32)
        pair = mine // 2

        def blend(at, carry):
            learned_ref[at] = base_ref[at] + polarity * shift_ref[pair, at]
            return carry

        lax.fori_loop(0, 6 * units, blend, 0, unroll=16)
        unroll_out[...] = losses_ref[mine][0:1, 0:1] / loss_count
        outer = jnp.zeros(outer_out.shape, jnp.float32)
        for q in range(npop // 2):
            differ = (losses_ref[2 * q] - losses_ref[2 * q + 1])[0:1, 0:1] / loss_count
            outer += differ * (accumulated_ref[q : q + 1, :] + perturbation_ref[q : q + 1, :])
        outer_out[...] = outer / (2 * (npop // 2))

    square = jnp.where(part == 0, stats_ref[0:1, 0:1], stats_ref[1:2, 0:1])
    scale = lax.rsqrt(square / count + grad_eps)

    @pl.loop(0, height // block)
    def _(at):
        here = pl.ds(pl.multiple_of(at * block, block), block)
        scaled = grad_ref[0, here, :] * scale
        first = beta_one * first_ref[0, 0, here, :] + (1.0 - beta_one) * scaled
        second = beta_two * second_ref[0, 0, here, :] + (1.0 - beta_two) * scaled * scaled
        first_out[0, 0, here, :] = first
        second_out[0, 0, here, :] = second
        inverse = lax.rsqrt(second)
        slope = scaled * inverse
        momentum = first * inverse
        held = weights_ref[0, 0, here, :]
        shift = momentum
        gate = jnp.zeros_like(momentum)
        for unit in range(units):
            hidden = jnp.tanh(
                slope * learned_ref[unit]
                + momentum * learned_ref[units + unit]
                + (held * learned_ref[2 * units + unit] + learned_ref[3 * units + unit])
            )
            shift = shift + hidden * learned_ref[4 * units + unit]
            gate = gate + hidden * learned_ref[5 * units + unit]
        weights_out[0, 0, here, :] = held - step_size * shift * jnp.exp(jnp.tanh(gate))


def update(base, perturbation, accumulated, stats, losses, grad, weights, first, second, npop,
           count, loss_count):
    _, _, rows, rank = weights.shape
    height = min(rows, 128)
    spec = pl.BlockSpec((1, 1, height, rank), lambda p, i: (0, p, i, 0))
    shape = jax.ShapeDtypeStruct(weights.shape, jnp.float32)
    scalars = pl.BlockSpec(memory_space=pltpu.SMEM)

    def whole(extent):
        return pl.BlockSpec(extent, lambda p, i: (0,) * len(extent))

    outer_shape = (1, base.shape[0])
    return pl.pallas_call(
        functools.partial(update_kernel, npop, count, loss_count),
        grid=(2, rows // height),
        out_shape=(
            shape,
            shape,
            shape,
            jax.ShapeDtypeStruct((1, 1), jnp.float32),
            jax.ShapeDtypeStruct(outer_shape, jnp.float32),
        ),
        in_specs=[
            scalars,
            scalars,
            whole(stats.shape),
            whole(losses.shape),
            whole(perturbation.shape),
            whole(accumulated.shape),
            pl.BlockSpec((1, height, rank), lambda p, i: (p, i, 0)),
            spec,
            spec,
            spec,
        ],
        out_specs=(spec, spec, spec, whole((1, 1)), whole(outer_shape)),
        scratch_shapes=[pltpu.SMEM(base.shape, jnp.float32)],
        name="update",
    )(base, perturbation, stats, losses, perturbation, accumulated, grad, weights, first, second)


def local(
    mesh_shape,
    tokens,
    targets,
    norm_gain,
    weights,
    first_moment,
    second_moment,
    learned_params,
    perturbation,
    accumulated,
):
    n, npop = mesh_shape["shard"], mesh_shape["pop"]
    token_rows, width = tokens.shape
    rank = weights.shape[-1]
    grad, stats, losses = exchange(mesh_shape, tokens, targets, norm_gain[None], weights)
    new_weights, new_first, new_second, unroll, outer = update(
        learned_params, perturbation, accumulated, stats, losses, grad, weights, first_moment,
        second_moment, npop, width * rank, token_rows * n * width,
    )
    return (new_weights, new_first, new_second, unroll[0], outer[0])


def solution(mesh):
    rows = P("pop", None, "shard", None)
    return jax.shard_map(
        functools.partial(local, dict(mesh.shape)),
        mesh=mesh,
        in_specs=(P("shard", None), P("shard", None), P(), rows, rows, rows, P(), P(), P()),
        out_specs=(rows, rows, rows, P("pop"), P()),
        check_vma=False,
    )
```

```python
import functools
import math

import jax
import jax.numpy as jnp
from jax import lax
from jax.experimental import pallas as pl
from jax.experimental.pallas import tpu as pltpu
from jax.sharding import PartitionSpec as P

step_size = 0.1
beta_one = 0.9
beta_two = 0.99
norm_eps = 1e-05
grad_eps = 1e-06

LANES = 128
MESH = pl.DeviceIdType.MESH


def grid_of(n):
    nx = max(1, math.isqrt(n // 2))
    while n % nx:
        nx -= 1
    return n // nx, nx


def shard_at(pos, nz, nx):
    x = pos // nz
    zz = pos % nz
    z = zz + (x % 2) * (nz - 1 - 2 * zz)
    return z * nx + x


def position_of(shard, nz, nx):
    x = shard % nx
    z = shard // nx
    zz = z + (x % 2) * (nz - 1 - 2 * z)
    return x * nz + zz


class Ring:
    def __init__(self, n, block, sends, recvs, far):
        self.n, self.block, self.sends, self.recvs = n, block, sends, recvs
        self.nz, self.nx = grid_of(n)
        self.pos = position_of(lax.axis_index("shard"), self.nz, self.nx)
        half = n // 2
        self.hops = (half, n - 1 - half) if far == 0 else (n - 1 - half, half)

    def shard(self, pos):
        return shard_at(lax.rem(pos + 2 * self.n, self.n), self.nz, self.nx)

    def copy(self, way, hop, arriving=False):
        sign = 1 if way == 0 else -1
        back = hop + 1 if arriving else hop
        ref = self.block(self.shard(self.pos - sign * back))
        at = way * (self.n // 2 + 1) + hop
        return pltpu.make_async_remote_copy(
            src_ref=ref,
            dst_ref=ref,
            send_sem=self.sends.at[at],
            recv_sem=self.recvs.at[at],
            device_id={"shard": self.shard(self.pos + sign)},
            device_id_type=MESH,
        )

    def step(self, hop):
        for way in (0, 1):
            if 1 <= hop <= self.hops[way]:
                self.copy(way, hop - 1, arriving=True).wait_recv()
            if hop < self.hops[way]:
                self.copy(way, hop).start()

    def drain(self):
        for way in (0, 1):
            for hop in range(self.hops[way]):
                self.copy(way, hop).wait_send()


class Direct:
    def __init__(self, axis, n, source, slot, sends, recvs):
        self.axis, self.n, self.source, self.slot = axis, n, source, slot
        self.sends, self.recvs = sends, recvs
        self.me = lax.axis_index(axis)

    def copy(self, off, arriving=False):
        to = lax.rem(self.me + off, self.n)
        owner = lax.rem(self.me + self.n - off, self.n) if arriving else self.me
        return pltpu.make_async_remote_copy(
            src_ref=self.source(to),
            dst_ref=self.slot(owner),
            send_sem=self.sends.at[off - 1],
            recv_sem=self.recvs.at[off - 1],
            device_id={self.axis: to},
            device_id_type=MESH,
        )

    def start(self):
        for off in range(1, self.n):
            self.copy(off).start()

    def wait_recv(self):
        for off in range(1, self.n):
            self.copy(off, arriving=True).wait_recv()

    def drain(self):
        for off in range(1, self.n):
            self.copy(off).wait_send()


class Share:
    def __init__(self, axis, group, piece, sends, recvs):
        self.axis, self.group, self.piece = axis, group, piece
        self.sends, self.recvs = sends, recvs
        me = lax.axis_index(axis)
        self.at = lax.rem(me, group)
        self.base = me - self.at

    def copy(self, off, arriving=False):
        owner = lax.rem(self.at + self.group - off, self.group) if arriving else self.at
        return pltpu.make_async_remote_copy(
            src_ref=self.piece(owner),
            dst_ref=self.piece(owner),
            send_sem=self.sends.at[off - 1],
            recv_sem=self.recvs.at[off - 1],
            device_id={self.axis: self.base + lax.rem(self.at + off, self.group)},
            device_id_type=MESH,
        )

    def start(self):
        for off in range(1, self.group):
            self.copy(off).start()

    def wait_recv(self):
        for off in range(1, self.group):
            self.copy(off, arriving=True).wait_recv()

    def drain(self):
        for off in range(1, self.group):
            self.copy(off).wait_send()


def group_of(npop, rows):
    group = 4
    while group > 1 and (npop % group or rows % (16 * group)):
        group //= 2
    return group


def total_of(values):
    return jnp.sum(jnp.sum(values, axis=0, keepdims=True), axis=1, keepdims=True)


def exchange_kernel(
    n,
    npop,
    tokens_hbm,
    targets_hbm,
    gain_hbm,
    weights_hbm,
    grad_ref,
    stats_ref,
    losses_ref,
    tokens_ref,
    targets_ref,
    gain_ref,
    weights_ref,
    load_sem,
    gathered,
    normed,
    columns,
    columns_in,
    active_all,
    back_all,
    loss_own,
    loss_in,
    square_own,
    square_in,
    pop_own,
    pop_in,
    ring_send,
    ring_recv,
    direct_send,
    direct_recv,
    pop_send,
    pop_recv,
    share_send,
    share_recv,
):
    me = lax.axis_index("shard")
    mine = lax.axis_index("pop")
    width = tokens_ref.shape[1]
    rows = width // n
    token_rows = tokens_ref.shape[0]
    rank = weights_ref.shape[-1]
    down_scale = width ** (-0.5)
    up_scale = rank ** (-0.5)

    loads = [
        pltpu.make_async_copy(source, target, load_sem.at[i])
        for i, (source, target) in enumerate(
            [
                (weights_hbm, weights_ref),
                (tokens_hbm, tokens_ref),
                (gain_hbm, gain_ref),
                (targets_hbm, targets_ref),
            ]
        )
    ]
    barrier = pltpu.get_barrier_semaphore()
    for load in loads:
        load.start()
    for off in range(1, n):
        pl.semaphore_signal(
            barrier, inc=1, device_id={"shard": lax.rem(me + off, n)}, device_id_type=MESH
        )
    for off in range(1, npop):
        pl.semaphore_signal(
            barrier, inc=1, device_id={"pop": lax.rem(mine + off, npop)}, device_id_type=MESH
        )

    def row_block(index):
        return pl.ds(pl.multiple_of(index * rows, rows), rows)

    loads[0].wait()
    for part in (0, 1):
        gathered[part, row_block(me), :] = weights_ref[0, part].astype(jnp.bfloat16)
    pl.semaphore_wait(barrier, n - 1 + npop - 1)

    rings = [
        Ring(n, block, ring_send.at[i], ring_recv.at[i], far)
        for i, (block, far) in enumerate(
            [
                (lambda s: gathered.at[0, row_block(s), :], 0),
                (lambda s: gathered.at[1, row_block(s), :], 1),
                (lambda s: active_all.at[s], 0),
                (lambda s: back_all.at[s], 1),
            ]
        )
    ]
    down_ring, up_ring, active_ring, back_ring = rings
    group = group_of(npop, rows)
    piece = rows // group

    def piece_at(start):
        return pl.ds(pl.multiple_of(start, piece), piece)

    share = Share(
        "pop", group, lambda q: columns_in.at[:, :, piece_at(q * piece), :],
        share_send, share_recv,
    )
    sub = share.at
    columns_out = Direct(
        "shard", n,
        lambda s: columns.at[:, piece_at(s * rows + sub * piece), :],
        lambda s: columns_in.at[:, s, piece_at(sub * piece), :],
        direct_send.at[0], direct_recv.at[0],
    )
    loss_out = Direct(
        "shard", n, lambda s: loss_own, lambda s: loss_in.at[s],
        direct_send.at[1], direct_recv.at[1],
    )
    square_out = Direct(
        "shard", n, lambda s: square_own, lambda s: square_in.at[s],
        direct_send.at[2], direct_recv.at[2],
    )
    pop_out = Direct(
        "pop", npop, lambda s: pop_own, lambda s: pop_in.at[s], pop_send, pop_recv
    )

    down_ring.step(0)
    up_ring.step(0)

    for load in loads[1:]:
        load.wait()
    chunk = 256
    squares = jnp.zeros((token_rows, LANES), jnp.float32)
    for at in range(0, width, LANES):
        values = tokens_ref[:, at : at + LANES].astype(jnp.float32)
        squares += values * values
    mean = jnp.sum(squares, axis=1, keepdims=True) / width
    inverse = lax.rsqrt(mean + norm_eps)
    for at in range(0, width, LANES):
        values = tokens_ref[:, at : at + LANES].astype(jnp.float32)
        values = values * inverse * gain_ref[:, at : at + LANES]
        normed[:, at : at + LANES] = values.astype(jnp.bfloat16)
        columns[0, at : at + LANES, :] = values.T.astype(jnp.bfloat16)
        for index, source in ((1, tokens_ref), (2, targets_ref)):
            values = source[:, at : at + LANES].astype(jnp.float32)
            columns[index, at : at + LANES, :] = values.T.astype(jnp.bfloat16)
    columns_out.start()
    for index in range(3):
        columns_in[index, me, piece_at(sub * piece), :] = columns[
            index, piece_at(me * rows + sub * piece), :
        ]

    last = n // 2
    for hop in range(1, last):
        down_ring.step(hop)
        up_ring.step(hop)
        if hop == min(2, last - 1):
            columns_out.wait_recv()
            share.start()
    down_ring.step(last)

    pre = jnp.zeros((token_rows, rank), jnp.float32)
    for at in range(0, width, chunk):
        pre += jnp.dot(
            normed[:, at : at + chunk],
            gathered[0, at : at + chunk, :],
            preferred_element_type=jnp.float32,
        )
    pre = pre * down_scale
    logistic = jax.nn.sigmoid(pre)
    active = (pre * logistic).astype(jnp.bfloat16)
    active_all[me] = active
    active_ring.step(0)
    slope = logistic * (1.0 + pre * (1.0 - logistic)) * up_scale
    up_ring.step(last)

    loss = jnp.zeros((1, 1), jnp.float32)
    back = jnp.zeros((token_rows, rank), jnp.float32)
    for at in range(0, width, chunk):
        held = gathered[1, at : at + chunk, :]
        branch = lax.dot_general(
            active, held, (((1,), (1,)), ((), ())), preferred_element_type=jnp.float32
        )
        residual = (
            tokens_ref[:, at : at + chunk].astype(jnp.float32)
            + branch * up_scale
            - targets_ref[:, at : at + chunk].astype(jnp.float32)
        )
        loss += total_of(residual * residual)
        double = 2.0 * residual
        back += jnp.dot(double.astype(jnp.bfloat16), held, preferred_element_type=jnp.float32)
    back_all[me] = (back * slope).astype(jnp.bfloat16)
    loss_own[...] = jnp.broadcast_to(loss, loss_own.shape)
    back_ring.step(0)
    active_ring.step(1)
    loss_out.start()
    loss_in[me] = loss_own[...]
    share.wait_recv()

    def add_block(owner, first):
        used = active_all[owner]
        branch = lax.dot_general(
            gathered[1, row_block(me), :], used, (((1,), (1,)), ((), ())),
            preferred_element_type=jnp.float32,
        )
        residual = (
            columns_in[1, owner].astype(jnp.float32)
            + branch * up_scale
            - columns_in[2, owner].astype(jnp.float32)
        )
        upstream = (2.0 * residual).astype(jnp.bfloat16)
        down = jnp.dot(
            columns_in[0, owner], back_all[owner], preferred_element_type=jnp.float32
        )
        up = jnp.dot(upstream, used, preferred_element_type=jnp.float32)
        if first:
            grad_ref[0], grad_ref[1] = down, up
        else:
            grad_ref[0] += down
            grad_ref[1] += up

    add_block(me, True)
    for hop in range(1, last + 1):
        back_ring.step(hop)
        if hop > 1:
            active_ring.step(hop)
        add_block(back_ring.shard(back_ring.pos - hop), False)
        if hop < n - hop:
            add_block(back_ring.shard(back_ring.pos + hop), False)

    sums = []
    for part in (0, 1):
        acc = grad_ref[part] * (down_scale, up_scale)[part]
        grad_ref[part] = acc
        sums.append(total_of(acc * acc))
    line = lax.broadcasted_iota(jnp.int32, square_own.shape, 0)
    square_own[...] = jnp.where(
        line == 0,
        jnp.broadcast_to(sums[0], square_own.shape),
        jnp.broadcast_to(sums[1], square_own.shape),
    )
    square_out.start()
    square_in[me] = square_own[...]
    loss_out.wait_recv()
    losses = loss_in[0]
    for j in range(1, n):
        losses += loss_in[j]
    pop_own[...] = losses
    pop_out.start()
    pop_in[mine] = losses
    square_out.wait_recv()
    both = square_in[0]
    for j in range(1, n):
        both += square_in[j]
    stats_ref[...] = both
    pop_out.wait_recv()
    losses_ref[...] = pop_in[...]
    for item in (*rings, columns_out, share, loss_out, square_out, pop_out):
        item.drain()


def exchange(mesh_shape, tokens, targets, gain, weights):
    n, npop = mesh_shape["shard"], mesh_shape["pop"]
    token_rows, width = tokens.shape
    rank = weights.shape[-1]
    rows = width // n
    wide, narrow = jnp.float32, jnp.bfloat16
    tile = (8, LANES)
    vmem = pl.BlockSpec(memory_space=pltpu.VMEM)
    anywhere = pl.BlockSpec(memory_space=pl.ANY)
    return pl.pallas_call(
        functools.partial(exchange_kernel, n, npop),
        out_shape=(
            jax.ShapeDtypeStruct((2, rows, rank), wide),
            jax.ShapeDtypeStruct(tile, wide),
            jax.ShapeDtypeStruct((npop, *tile), wide),
        ),
        in_specs=[anywhere] * 4,
        out_specs=(vmem, vmem, vmem),
        scratch_shapes=[
            pltpu.VMEM(tokens.shape, tokens.dtype),
            pltpu.VMEM(targets.shape, targets.dtype),
            pltpu.VMEM(gain.shape, gain.dtype),
            pltpu.VMEM(weights.shape, weights.dtype),
            pltpu.SemaphoreType.DMA((4,)),
            pltpu.VMEM((2, width, rank), narrow),
            pltpu.VMEM((token_rows, width), narrow),
            pltpu.VMEM((3, width, token_rows), narrow),
            pltpu.VMEM((3, n, rows, token_rows), narrow),
            pltpu.VMEM((n, token_rows, rank), narrow),
            pltpu.VMEM((n, token_rows, rank), narrow),
            pltpu.VMEM(tile, wide),
            pltpu.VMEM((n, *tile), wide),
            pltpu.VMEM(tile, wide),
            pltpu.VMEM((n, *tile), wide),
            pltpu.VMEM(tile, wide),
            pltpu.VMEM((npop, *tile), wide),
            pltpu.SemaphoreType.DMA((4, n + 2)),
            pltpu.SemaphoreType.DMA((4, n + 2)),
            pltpu.SemaphoreType.DMA((3, n)),
            pltpu.SemaphoreType.DMA((3, n)),
            pltpu.SemaphoreType.DMA((npop,)),
            pltpu.SemaphoreType.DMA((npop,)),
            pltpu.SemaphoreType.DMA((4,)),
            pltpu.SemaphoreType.DMA((4,)),
        ],
        compiler_params=pltpu.CompilerParams(
            collective_id=0, has_side_effects=True
        ),
        name="exchange",
    )(tokens, targets, gain, weights)


def update_kernel(
    npop, count, loss_count, base_ref, shift_ref, stats_ref, losses_ref, perturbation_ref,
    accumulated_ref, grad_ref, weights_ref, first_ref, second_ref,
    weights_out, first_out, second_out, unroll_out, outer_out, learned_ref,
):
    part = pl.program_id(0)
    mine = lax.axis_index("pop")
    units = base_ref.shape[0] // 6
    height = grad_ref.shape[1]
    block = min(32, height)

    @pl.when((part == 0) & (pl.program_id(1) == 0))
    def _():
        polarity = (1 - 2 * lax.rem(mine, 2)).astype(jnp.float32)
        pair = mine // 2

        def blend(at, carry):
            learned_ref[at] = base_ref[at] + polarity * shift_ref[pair, at]
            return carry

        lax.fori_loop(0, 6 * units, blend, 0, unroll=16)
        unroll_out[...] = losses_ref[mine][0:1, 0:1] / loss_count
        outer = jnp.zeros(outer_out.shape, jnp.float32)
        for q in range(npop // 2):
            differ = (losses_ref[2 * q] - losses_ref[2 * q + 1])[0:1, 0:1] / loss_count
            outer += differ * (accumulated_ref[q : q + 1, :] + perturbation_ref[q : q + 1, :])
        outer_out[...] = outer / (2 * (npop // 2))

    square = jnp.where(part == 0, stats_ref[0:1, 0:1], stats_ref[1:2, 0:1])
    scale = lax.rsqrt(square / count + grad_eps)

    @pl.loop(0, height // block)
    def _(at):
        here = pl.ds(pl.multiple_of(at * block, block), block)
        scaled = grad_ref[0, here, :] * scale
        first = beta_one * first_ref[0, 0, here, :] + (1.0 - beta_one) * scaled
        second = beta_two * second_ref[0, 0, here, :] + (1.0 - beta_two) * scaled * scaled
        first_out[0, 0, here, :] = first
        second_out[0, 0, here, :] = second
        inverse = lax.rsqrt(second)
        slope = scaled * inverse
        momentum = first * inverse
        held = weights_ref[0, 0, here, :]
        shift = momentum
        gate = jnp.zeros_like(momentum)
        for unit in range(units):
            hidden = jnp.tanh(
                slope * learned_ref[unit]
                + momentum * learned_ref[units + unit]
                + (held * learned_ref[2 * units + unit] + learned_ref[3 * units + unit])
            )
            shift = shift + hidden * learned_ref[4 * units + unit]
            gate = gate + hidden * learned_ref[5 * units + unit]
        weights_out[0, 0, here, :] = held - step_size * shift * jnp.exp(jnp.tanh(gate))


def update(base, perturbation, accumulated, stats, losses, grad, weights, first, second, npop,
           count, loss_count):
    _, _, rows, rank = weights.shape
    height = min(rows, 128)
    spec = pl.BlockSpec((1, 1, height, rank), lambda p, i: (0, p, i, 0))
    shape = jax.ShapeDtypeStruct(weights.shape, jnp.float32)
    scalars = pl.BlockSpec(memory_space=pltpu.SMEM)

    def whole(extent):
        return pl.BlockSpec(extent, lambda p, i: (0,) * len(extent))

    outer_shape = (1, base.shape[0])
    return pl.pallas_call(
        functools.partial(update_kernel, npop, count, loss_count),
        grid=(2, rows // height),
        out_shape=(
            shape,
            shape,
            shape,
            jax.ShapeDtypeStruct((1, 1), jnp.float32),
            jax.ShapeDtypeStruct(outer_shape, jnp.float32),
        ),
        in_specs=[
            scalars,
            scalars,
            whole(stats.shape),
            whole(losses.shape),
            whole(perturbation.shape),
            whole(accumulated.shape),
            pl.BlockSpec((1, height, rank), lambda p, i: (p, i, 0)),
            spec,
            spec,
            spec,
        ],
        out_specs=(spec, spec, spec, whole((1, 1)), whole(outer_shape)),
        scratch_shapes=[pltpu.SMEM(base.shape, jnp.float32)],
        name="update",
    )(base, perturbation, stats, losses, perturbation, accumulated, grad, weights, first, second)


def local(
    mesh_shape,
    tokens,
    targets,
    norm_gain,
    weights,
    first_moment,
    second_moment,
    learned_params,
    perturbation,
    accumulated,
):
    n, npop = mesh_shape["shard"], mesh_shape["pop"]
    token_rows, width = tokens.shape
    rank = weights.shape[-1]
    grad, stats, losses = exchange(mesh_shape, tokens, targets, norm_gain[None], weights)
    new_weights, new_first, new_second, unroll, outer = update(
        learned_params, perturbation, accumulated, stats, losses, grad, weights, first_moment,
        second_moment, npop, width * rank, token_rows * n * width,
    )
    return (new_weights, new_first, new_second, unroll[0], outer[0])


def solution(mesh):
    rows = P("pop", None, "shard", None)
    return jax.shard_map(
        functools.partial(local, dict(mesh.shape)),
        mesh=mesh,
        in_specs=(P("shard", None), P("shard", None), P(), rows, rows, rows, P(), P(), P()),
        out_specs=(rows, rows, rows, P("pop"), P()),
        check_vma=False,
    )
```

```python
import functools
import math

import jax
import jax.numpy as jnp
from jax import lax
from jax.experimental import pallas as pl
from jax.experimental.pallas import tpu as pltpu
from jax.sharding import PartitionSpec as P

step_size = 0.1
beta_one = 0.9
beta_two = 0.99
norm_eps = 1e-05
grad_eps = 1e-06

LANES = 128
MESH = pl.DeviceIdType.MESH


def grid_of(n):
    nx = max(1, math.isqrt(n // 2))
    while n % nx:
        nx -= 1
    return n // nx, nx


def shard_at(pos, nz, nx):
    x = pos // nz
    zz = pos % nz
    z = zz + (x % 2) * (nz - 1 - 2 * zz)
    return z * nx + x


def position_of(shard, nz, nx):
    x = shard % nx
    z = shard // nx
    zz = z + (x % 2) * (nz - 1 - 2 * z)
    return x * nz + zz


class Ring:
    def __init__(self, n, block, sends, recvs, far):
        self.n, self.block, self.sends, self.recvs = n, block, sends, recvs
        self.nz, self.nx = grid_of(n)
        self.pos = position_of(lax.axis_index("shard"), self.nz, self.nx)
        half = n // 2
        self.hops = (half, n - 1 - half) if far == 0 else (n - 1 - half, half)

    def shard(self, pos):
        return shard_at(lax.rem(pos + 2 * self.n, self.n), self.nz, self.nx)

    def copy(self, way, hop, arriving=False):
        sign = 1 if way == 0 else -1
        back = hop + 1 if arriving else hop
        ref = self.block(self.shard(self.pos - sign * back))
        at = way * (self.n // 2 + 1) + hop
        return pltpu.make_async_remote_copy(
            src_ref=ref,
            dst_ref=ref,
            send_sem=self.sends.at[at],
            recv_sem=self.recvs.at[at],
            device_id={"shard": self.shard(self.pos + sign)},
            device_id_type=MESH,
        )

    def step(self, hop):
        for way in (0, 1):
            if 1 <= hop <= self.hops[way]:
                self.copy(way, hop - 1, arriving=True).wait_recv()
            if hop < self.hops[way]:
                self.copy(way, hop).start()

    def drain(self):
        for way in (0, 1):
            for hop in range(self.hops[way]):
                self.copy(way, hop).wait_send()


class Direct:
    def __init__(self, axis, n, source, slot, sends, recvs):
        self.axis, self.n, self.source, self.slot = axis, n, source, slot
        self.sends, self.recvs = sends, recvs
        self.me = lax.axis_index(axis)

    def copy(self, off, arriving=False):
        to = lax.rem(self.me + off, self.n)
        owner = lax.rem(self.me + self.n - off, self.n) if arriving else self.me
        return pltpu.make_async_remote_copy(
            src_ref=self.source(to),
            dst_ref=self.slot(owner),
            send_sem=self.sends.at[off - 1],
            recv_sem=self.recvs.at[off - 1],
            device_id={self.axis: to},
            device_id_type=MESH,
        )

    def start(self):
        for off in range(1, self.n):
            self.copy(off).start()

    def wait_recv(self):
        for off in range(1, self.n):
            self.copy(off, arriving=True).wait_recv()

    def drain(self):
        for off in range(1, self.n):
            self.copy(off).wait_send()


class Share:
    def __init__(self, axis, group, piece, sends, recvs):
        self.axis, self.group, self.piece = axis, group, piece
        self.sends, self.recvs = sends, recvs
        me = lax.axis_index(axis)
        self.at = lax.rem(me, group)
        self.base = me - self.at
        self.partner = self.at + 1 - 2 * lax.rem(self.at, 2)
        self.across = lax.rem(self.at + 2, 4)

    def copy(self, kind, arriving=False):
        if arriving:
            owner = (self.across, self.partner, lax.rem(self.partner + 2, 4))[kind]
        else:
            owner = (self.at, self.at, self.across)[kind]
        to = self.across if kind == 0 else self.partner
        return pltpu.make_async_remote_copy(
            src_ref=self.piece(owner),
            dst_ref=self.piece(owner),
            send_sem=self.sends.at[kind],
            recv_sem=self.recvs.at[kind],
            device_id={self.axis: self.base + to},
            device_id_type=MESH,
        )

    def start(self):
        if self.group == 4:
            self.copy(0).start()
            self.copy(1).start()

    def relay(self):
        if self.group == 4:
            self.copy(0, arriving=True).wait_recv()
            self.copy(2).start()

    def wait_recv(self):
        if self.group == 4:
            self.copy(1, arriving=True).wait_recv()
            self.copy(2, arriving=True).wait_recv()

    def drain(self):
        if self.group == 4:
            for kind in range(3):
                self.copy(kind).wait_send()


def group_of(npop, rows):
    return 1 if npop % 4 or rows % 64 else 4


def total_of(values):
    return jnp.sum(jnp.sum(values, axis=0, keepdims=True), axis=1, keepdims=True)


def exchange_kernel(
    n,
    npop,
    tokens_hbm,
    targets_hbm,
    gain_hbm,
    weights_hbm,
    grad_ref,
    stats_ref,
    losses_ref,
    tokens_ref,
    targets_ref,
    gain_ref,
    weights_ref,
    load_sem,
    gathered,
    normed,
    columns,
    columns_in,
    gain_t,
    scale_own,
    scale_in,
    active_all,
    back_all,
    loss_own,
    loss_in,
    square_own,
    square_in,
    pop_own,
    pop_in,
    ring_send,
    ring_recv,
    direct_send,
    direct_recv,
    pop_send,
    pop_recv,
    share_send,
    share_recv,
):
    me = lax.axis_index("shard")
    mine = lax.axis_index("pop")
    width = tokens_ref.shape[1]
    rows = width // n
    token_rows = tokens_ref.shape[0]
    rank = weights_ref.shape[-1]
    down_scale = width ** (-0.5)
    up_scale = rank ** (-0.5)

    loads = [
        pltpu.make_async_copy(source, target, load_sem.at[i])
        for i, (source, target) in enumerate(
            [
                (weights_hbm, weights_ref),
                (tokens_hbm, tokens_ref),
                (gain_hbm, gain_ref),
                (targets_hbm, targets_ref),
            ]
        )
    ]
    barrier = pltpu.get_barrier_semaphore()
    for load in loads:
        load.start()
    for off in range(1, n):
        pl.semaphore_signal(
            barrier, inc=1, device_id={"shard": lax.rem(me + off, n)}, device_id_type=MESH
        )
    for off in range(1, npop):
        pl.semaphore_signal(
            barrier, inc=1, device_id={"pop": lax.rem(mine + off, npop)}, device_id_type=MESH
        )

    def row_block(index):
        return pl.ds(pl.multiple_of(index * rows, rows), rows)

    loads[0].wait()
    for part in (0, 1):
        gathered[part, row_block(me), :] = weights_ref[0, part].astype(jnp.bfloat16)
    pl.semaphore_wait(barrier, n - 1 + npop - 1)

    rings = [
        Ring(n, block, ring_send.at[i], ring_recv.at[i], far)
        for i, (block, far) in enumerate(
            [
                (lambda s: gathered.at[0, row_block(s), :], 0),
                (lambda s: gathered.at[1, row_block(s), :], 1),
                (lambda s: active_all.at[s], 0),
                (lambda s: back_all.at[s], 1),
            ]
        )
    ]
    down_ring, up_ring, active_ring, back_ring = rings
    group = group_of(npop, rows)
    piece = rows // group

    def piece_at(start):
        return pl.ds(pl.multiple_of(start, piece), piece)

    share = Share(
        "pop", group, lambda q: columns_in.at[:, :, piece_at(q * piece), :],
        share_send, share_recv,
    )
    sub = share.at
    columns_out = Direct(
        "shard", n,
        lambda s: columns.at[:, piece_at(s * rows + sub * piece), :],
        lambda s: columns_in.at[:, s, piece_at(sub * piece), :],
        direct_send.at[0], direct_recv.at[0],
    )
    loss_out = Direct(
        "shard", n, lambda s: loss_own, lambda s: loss_in.at[s],
        direct_send.at[1], direct_recv.at[1],
    )
    square_out = Direct(
        "shard", n, lambda s: square_own, lambda s: square_in.at[s],
        direct_send.at[2], direct_recv.at[2],
    )
    scale_out = Direct(
        "shard", n, lambda s: scale_own, lambda s: scale_in.at[s],
        direct_send.at[3], direct_recv.at[3],
    )
    pop_out = Direct(
        "pop", npop, lambda s: pop_own, lambda s: pop_in.at[s], pop_send, pop_recv
    )

    down_ring.step(0)
    up_ring.step(0)

    for load in loads[1:]:
        load.wait()
    chunk = 256
    for at in range(0, width, LANES):
        for index, source in enumerate((tokens_ref, targets_ref)):
            values = source[:, at : at + LANES].astype(jnp.float32)
            columns[index, at : at + LANES, :] = values.T.astype(jnp.bfloat16)
    columns_out.start()
    for index in range(2):
        columns_in[index, me, piece_at(sub * piece), :] = columns[
            index, piece_at(me * rows + sub * piece), :
        ]
    squares = jnp.zeros((token_rows, LANES), jnp.float32)
    for at in range(0, width, LANES):
        values = tokens_ref[:, at : at + LANES].astype(jnp.float32)
        squares += values * values
    mean = jnp.sum(squares, axis=1, keepdims=True) / width
    inverse = lax.rsqrt(mean + norm_eps)
    scale_own[...] = jnp.broadcast_to(inverse, (token_rows, LANES)).T[0:8]
    for at in range(0, width, LANES):
        values = tokens_ref[:, at : at + LANES].astype(jnp.float32)
        gain = gain_ref[:, at : at + LANES]
        normed[:, at : at + LANES] = (values * inverse * gain).astype(jnp.bfloat16)
        gain_t[at : at + LANES, :] = jnp.broadcast_to(gain, (token_rows, LANES)).T
    scale_out.start()
    scale_in[me] = scale_own[...]

    last = n // 2
    for hop in range(1, last):
        down_ring.step(hop)
        up_ring.step(hop)
        if hop == min(2, last - 1):
            columns_out.wait_recv()
            share.start()
    down_ring.step(last)

    pre = jnp.zeros((token_rows, rank), jnp.float32)
    for at in range(0, width, chunk):
        pre += jnp.dot(
            normed[:, at : at + chunk],
            gathered[0, at : at + chunk, :],
            preferred_element_type=jnp.float32,
        )
    pre = pre * down_scale
    logistic = jax.nn.sigmoid(pre)
    active = (pre * logistic).astype(jnp.bfloat16)
    active_all[me] = active
    active_ring.step(0)
    share.relay()
    slope = logistic * (1.0 + pre * (1.0 - logistic)) * up_scale
    up_ring.step(last)

    loss = jnp.zeros((1, 1), jnp.float32)
    back = jnp.zeros((token_rows, rank), jnp.float32)
    for at in range(0, width, chunk):
        held = gathered[1, at : at + chunk, :]
        branch = lax.dot_general(
            active, held, (((1,), (1,)), ((), ())), preferred_element_type=jnp.float32
        )
        residual = (
            tokens_ref[:, at : at + chunk].astype(jnp.float32)
            + branch * up_scale
            - targets_ref[:, at : at + chunk].astype(jnp.float32)
        )
        loss += total_of(residual * residual)
        double = 2.0 * residual
        back += jnp.dot(double.astype(jnp.bfloat16), held, preferred_element_type=jnp.float32)
    back_all[me] = (back * slope).astype(jnp.bfloat16)
    loss_own[...] = jnp.broadcast_to(loss, loss_own.shape)
    back_ring.step(0)
    active_ring.step(1)
    loss_out.start()
    loss_in[me] = loss_own[...]
    share.wait_recv()
    scale_out.wait_recv()

    def add_block(owner, first):
        used = active_all[owner]
        branch = lax.dot_general(
            gathered[1, row_block(me), :], used, (((1,), (1,)), ((), ())),
            preferred_element_type=jnp.float32,
        )
        residual = (
            columns_in[0, owner].astype(jnp.float32)
            + branch * up_scale
            - columns_in[1, owner].astype(jnp.float32)
        )
        upstream = (2.0 * residual).astype(jnp.bfloat16)
        scaled = columns_in[0, owner].astype(jnp.float32) * scale_in[owner][0:1, :]
        scaled = (scaled * gain_t[row_block(me), :]).astype(jnp.bfloat16)
        down = jnp.dot(scaled, back_all[owner], preferred_element_type=jnp.float32)
        up = jnp.dot(upstream, used, preferred_element_type=jnp.float32)
        if first:
            grad_ref[0], grad_ref[1] = down, up
        else:
            grad_ref[0] += down
            grad_ref[1] += up

    add_block(me, True)
    for hop in range(1, last + 1):
        back_ring.step(hop)
        if hop > 1:
            active_ring.step(hop)
        add_block(back_ring.shard(back_ring.pos - hop), False)
        if hop < n - hop:
            add_block(back_ring.shard(back_ring.pos + hop), False)

    sums = []
    for part in (0, 1):
        acc = grad_ref[part] * (down_scale, up_scale)[part]
        grad_ref[part] = acc
        sums.append(total_of(acc * acc))
    line = lax.broadcasted_iota(jnp.int32, square_own.shape, 0)
    square_own[...] = jnp.where(
        line == 0,
        jnp.broadcast_to(sums[0], square_own.shape),
        jnp.broadcast_to(sums[1], square_own.shape),
    )
    square_out.start()
    square_in[me] = square_own[...]
    loss_out.wait_recv()
    losses = loss_in[0]
    for j in range(1, n):
        losses += loss_in[j]
    pop_own[...] = losses
    pop_out.start()
    pop_in[mine] = losses
    square_out.wait_recv()
    both = square_in[0]
    for j in range(1, n):
        both += square_in[j]
    stats_ref[...] = both
    pop_out.wait_recv()
    losses_ref[...] = pop_in[...]
    for item in (*rings, columns_out, share, scale_out, loss_out, square_out, pop_out):
        item.drain()


def exchange(mesh_shape, tokens, targets, gain, weights):
    n, npop = mesh_shape["shard"], mesh_shape["pop"]
    token_rows, width = tokens.shape
    rank = weights.shape[-1]
    rows = width // n
    wide, narrow = jnp.float32, jnp.bfloat16
    tile = (8, LANES)
    vmem = pl.BlockSpec(memory_space=pltpu.VMEM)
    anywhere = pl.BlockSpec(memory_space=pl.ANY)
    return pl.pallas_call(
        functools.partial(exchange_kernel, n, npop),
        out_shape=(
            jax.ShapeDtypeStruct((2, rows, rank), wide),
            jax.ShapeDtypeStruct(tile, wide),
            jax.ShapeDtypeStruct((npop, *tile), wide),
        ),
        in_specs=[anywhere] * 4,
        out_specs=(vmem, vmem, vmem),
        scratch_shapes=[
            pltpu.VMEM(tokens.shape, tokens.dtype),
            pltpu.VMEM(targets.shape, targets.dtype),
            pltpu.VMEM(gain.shape, gain.dtype),
            pltpu.VMEM(weights.shape, weights.dtype),
            pltpu.SemaphoreType.DMA((4,)),
            pltpu.VMEM((2, width, rank), narrow),
            pltpu.VMEM((token_rows, width), narrow),
            pltpu.VMEM((2, width, token_rows), narrow),
            pltpu.VMEM((2, n, rows, token_rows), narrow),
            pltpu.VMEM((width, token_rows), wide),
            pltpu.VMEM((8, token_rows), wide),
            pltpu.VMEM((n, 8, token_rows), wide),
            pltpu.VMEM((n, token_rows, rank), narrow),
            pltpu.VMEM((n, token_rows, rank), narrow),
            pltpu.VMEM(tile, wide),
            pltpu.VMEM((n, *tile), wide),
            pltpu.VMEM(tile, wide),
            pltpu.VMEM((n, *tile), wide),
            pltpu.VMEM(tile, wide),
            pltpu.VMEM((npop, *tile), wide),
            pltpu.SemaphoreType.DMA((4, n + 2)),
            pltpu.SemaphoreType.DMA((4, n + 2)),
            pltpu.SemaphoreType.DMA((4, n)),
            pltpu.SemaphoreType.DMA((4, n)),
            pltpu.SemaphoreType.DMA((npop,)),
            pltpu.SemaphoreType.DMA((npop,)),
            pltpu.SemaphoreType.DMA((4,)),
            pltpu.SemaphoreType.DMA((4,)),
        ],
        compiler_params=pltpu.CompilerParams(
            collective_id=0, has_side_effects=True
        ),
        name="exchange",
    )(tokens, targets, gain, weights)


def update_kernel(
    npop, count, loss_count, base_ref, shift_ref, stats_ref, losses_ref, perturbation_ref,
    accumulated_ref, grad_ref, weights_ref, first_ref, second_ref,
    weights_out, first_out, second_out, unroll_out, outer_out, learned_ref,
):
    part = pl.program_id(0)
    mine = lax.axis_index("pop")
    units = base_ref.shape[0] // 6
    height = grad_ref.shape[1]
    block = min(32, height)

    @pl.when((part == 0) & (pl.program_id(1) == 0))
    def _():
        polarity = (1 - 2 * lax.rem(mine, 2)).astype(jnp.float32)
        pair = mine // 2

        def blend(at, carry):
            learned_ref[at] = base_ref[at] + polarity * shift_ref[pair, at]
            return carry

        lax.fori_loop(0, 6 * units, blend, 0, unroll=16)
        unroll_out[...] = losses_ref[mine][0:1, 0:1] / loss_count
        outer = jnp.zeros(outer_out.shape, jnp.float32)
        for q in range(npop // 2):
            differ = (losses_ref[2 * q] - losses_ref[2 * q + 1])[0:1, 0:1] / loss_count
            outer += differ * (accumulated_ref[q : q + 1, :] + perturbation_ref[q : q + 1, :])
        outer_out[...] = outer / (2 * (npop // 2))

    square = jnp.where(part == 0, stats_ref[0:1, 0:1], stats_ref[1:2, 0:1])
    scale = lax.rsqrt(square / count + grad_eps)

    @pl.loop(0, height // block)
    def _(at):
        here = pl.ds(pl.multiple_of(at * block, block), block)
        scaled = grad_ref[0, here, :] * scale
        first = beta_one * first_ref[0, 0, here, :] + (1.0 - beta_one) * scaled
        second = beta_two * second_ref[0, 0, here, :] + (1.0 - beta_two) * scaled * scaled
        first_out[0, 0, here, :] = first
        second_out[0, 0, here, :] = second
        inverse = lax.rsqrt(second)
        slope = scaled * inverse
        momentum = first * inverse
        held = weights_ref[0, 0, here, :]
        shift = momentum
        gate = jnp.zeros_like(momentum)
        for unit in range(units):
            hidden = jnp.tanh(
                slope * learned_ref[unit]
                + momentum * learned_ref[units + unit]
                + (held * learned_ref[2 * units + unit] + learned_ref[3 * units + unit])
            )
            shift = shift + hidden * learned_ref[4 * units + unit]
            gate = gate + hidden * learned_ref[5 * units + unit]
        weights_out[0, 0, here, :] = held - step_size * shift * jnp.exp(jnp.tanh(gate))


def update(base, perturbation, accumulated, stats, losses, grad, weights, first, second, npop,
           count, loss_count):
    _, _, rows, rank = weights.shape
    height = min(rows, 128)
    spec = pl.BlockSpec((1, 1, height, rank), lambda p, i: (0, p, i, 0))
    shape = jax.ShapeDtypeStruct(weights.shape, jnp.float32)
    scalars = pl.BlockSpec(memory_space=pltpu.SMEM)

    def whole(extent):
        return pl.BlockSpec(extent, lambda p, i: (0,) * len(extent))

    outer_shape = (1, base.shape[0])
    return pl.pallas_call(
        functools.partial(update_kernel, npop, count, loss_count),
        grid=(2, rows // height),
        out_shape=(
            shape,
            shape,
            shape,
            jax.ShapeDtypeStruct((1, 1), jnp.float32),
            jax.ShapeDtypeStruct(outer_shape, jnp.float32),
        ),
        in_specs=[
            scalars,
            scalars,
            whole(stats.shape),
            whole(losses.shape),
            whole(perturbation.shape),
            whole(accumulated.shape),
            pl.BlockSpec((1, height, rank), lambda p, i: (p, i, 0)),
            spec,
            spec,
            spec,
        ],
        out_specs=(spec, spec, spec, whole((1, 1)), whole(outer_shape)),
        scratch_shapes=[pltpu.SMEM(base.shape, jnp.float32)],
        name="update",
    )(base, perturbation, stats, losses, perturbation, accumulated, grad, weights, first, second)


def local(
    mesh_shape,
    tokens,
    targets,
    norm_gain,
    weights,
    first_moment,
    second_moment,
    learned_params,
    perturbation,
    accumulated,
):
    n, npop = mesh_shape["shard"], mesh_shape["pop"]
    token_rows, width = tokens.shape
    rank = weights.shape[-1]
    grad, stats, losses = exchange(mesh_shape, tokens, targets, norm_gain[None], weights)
    new_weights, new_first, new_second, unroll, outer = update(
        learned_params, perturbation, accumulated, stats, losses, grad, weights, first_moment,
        second_moment, npop, width * rank, token_rows * n * width,
    )
    return (new_weights, new_first, new_second, unroll[0], outer[0])


def solution(mesh):
    rows = P("pop", None, "shard", None)
    return jax.shard_map(
        functools.partial(local, dict(mesh.shape)),
        mesh=mesh,
        in_specs=(P("shard", None), P("shard", None), P(), rows, rows, rows, P(), P(), P()),
        out_specs=(rows, rows, rows, P("pop"), P()),
        check_vma=False,
    )
```

```python
import functools
import math

import jax
import jax.numpy as jnp
from jax import lax
from jax.experimental import pallas as pl
from jax.experimental.pallas import tpu as pltpu
from jax.sharding import PartitionSpec as P

step_size = 0.1
beta_one = 0.9
beta_two = 0.99
norm_eps = 1e-05
grad_eps = 1e-06

LANES = 128
MESH = pl.DeviceIdType.MESH


def grid_of(n):
    nx = max(1, math.isqrt(n // 2))
    while n % nx:
        nx -= 1
    return n // nx, nx


def shard_at(pos, nz, nx):
    x = pos // nz
    zz = pos % nz
    z = zz + (x % 2) * (nz - 1 - 2 * zz)
    return z * nx + x


def position_of(shard, nz, nx):
    x = shard % nx
    z = shard // nx
    zz = z + (x % 2) * (nz - 1 - 2 * z)
    return x * nz + zz


class Ring:
    def __init__(self, n, block, sends, recvs, far):
        self.n, self.block, self.sends, self.recvs = n, block, sends, recvs
        self.nz, self.nx = grid_of(n)
        self.pos = position_of(lax.axis_index("shard"), self.nz, self.nx)
        half = n // 2
        self.hops = (half, n - 1 - half) if far == 0 else (n - 1 - half, half)

    def shard(self, pos):
        return shard_at(lax.rem(pos + 2 * self.n, self.n), self.nz, self.nx)

    def copy(self, way, hop, arriving=False):
        sign = 1 if way == 0 else -1
        back = hop + 1 if arriving else hop
        ref = self.block(self.shard(self.pos - sign * back))
        at = way * (self.n // 2 + 1) + hop
        return pltpu.make_async_remote_copy(
            src_ref=ref,
            dst_ref=ref,
            send_sem=self.sends.at[at],
            recv_sem=self.recvs.at[at],
            device_id={"shard": self.shard(self.pos + sign)},
            device_id_type=MESH,
        )

    def step(self, hop):
        for way in (0, 1):
            if 1 <= hop <= self.hops[way]:
                self.copy(way, hop - 1, arriving=True).wait_recv()
            if hop < self.hops[way]:
                self.copy(way, hop).start()

    def drain(self):
        for way in (0, 1):
            for hop in range(self.hops[way]):
                self.copy(way, hop).wait_send()


class Halves:
    def __init__(self, n, block, sends, recvs):
        self.rings = [
            Ring(n, functools.partial(block, half), sends.at[half], recvs.at[half], half)
            for half in (0, 1)
        ]
        self.shard, self.pos = self.rings[0].shard, self.rings[0].pos

    def step(self, hop):
        for ring in self.rings:
            ring.step(hop)

    def drain(self):
        for ring in self.rings:
            ring.drain()


class Direct:
    def __init__(self, axis, n, source, slot, sends, recvs):
        self.axis, self.n, self.source, self.slot = axis, n, source, slot
        self.sends, self.recvs = sends, recvs
        self.me = lax.axis_index(axis)

    def copy(self, off, arriving=False):
        to = lax.rem(self.me + off, self.n)
        owner = lax.rem(self.me + self.n - off, self.n) if arriving else self.me
        return pltpu.make_async_remote_copy(
            src_ref=self.source(to),
            dst_ref=self.slot(owner),
            send_sem=self.sends.at[off - 1],
            recv_sem=self.recvs.at[off - 1],
            device_id={self.axis: to},
            device_id_type=MESH,
        )

    def start(self):
        for off in range(1, self.n):
            self.copy(off).start()

    def wait_recv(self):
        for off in range(1, self.n):
            self.copy(off, arriving=True).wait_recv()

    def drain(self):
        for off in range(1, self.n):
            self.copy(off).wait_send()


class Share:
    def __init__(self, axis, group, piece, sends, recvs):
        self.axis, self.group, self.piece = axis, group, piece
        self.sends, self.recvs = sends, recvs
        me = lax.axis_index(axis)
        self.at = lax.rem(me, group)
        self.base = me - self.at
        self.partner = self.at + 1 - 2 * lax.rem(self.at, 2)
        self.across = lax.rem(self.at + 2, 4)

    def copy(self, kind, arriving=False):
        if arriving:
            owner = (self.across, self.partner, lax.rem(self.partner + 2, 4))[kind]
        else:
            owner = (self.at, self.at, self.across)[kind]
        to = self.across if kind == 0 else self.partner
        return pltpu.make_async_remote_copy(
            src_ref=self.piece(owner),
            dst_ref=self.piece(owner),
            send_sem=self.sends.at[kind],
            recv_sem=self.recvs.at[kind],
            device_id={self.axis: self.base + to},
            device_id_type=MESH,
        )

    def start(self):
        if self.group == 4:
            self.copy(0).start()
            self.copy(1).start()

    def relay(self):
        if self.group == 4:
            self.copy(0, arriving=True).wait_recv()
            self.copy(2).start()

    def wait_recv(self):
        if self.group == 4:
            self.copy(1, arriving=True).wait_recv()
            self.copy(2, arriving=True).wait_recv()

    def drain(self):
        if self.group == 4:
            for kind in range(3):
                self.copy(kind).wait_send()


def group_of(npop, rows):
    return 1 if npop % 4 or rows % 64 else 4


def total_of(values):
    return jnp.sum(jnp.sum(values, axis=0, keepdims=True), axis=1, keepdims=True)


def exchange_kernel(
    n,
    npop,
    tokens_hbm,
    targets_hbm,
    gain_hbm,
    weights_hbm,
    grad_ref,
    stats_ref,
    losses_ref,
    tokens_ref,
    targets_ref,
    gain_ref,
    weights_ref,
    load_sem,
    gathered,
    normed,
    columns,
    columns_in,
    gain_t,
    scale_own,
    scale_in,
    active_all,
    back_all,
    loss_own,
    loss_in,
    square_own,
    square_in,
    pop_own,
    pop_in,
    ring_send,
    ring_recv,
    direct_send,
    direct_recv,
    pop_send,
    pop_recv,
    share_send,
    share_recv,
):
    me = lax.axis_index("shard")
    mine = lax.axis_index("pop")
    width = tokens_ref.shape[1]
    rows = width // n
    token_rows = tokens_ref.shape[0]
    rank = weights_ref.shape[-1]
    down_scale = width ** (-0.5)
    up_scale = rank ** (-0.5)

    loads = [
        pltpu.make_async_copy(source, target, load_sem.at[i])
        for i, (source, target) in enumerate(
            [
                (weights_hbm, weights_ref),
                (tokens_hbm, tokens_ref),
                (gain_hbm, gain_ref),
                (targets_hbm, targets_ref),
            ]
        )
    ]
    barrier = pltpu.get_barrier_semaphore()
    for load in loads:
        load.start()
    for off in range(1, n):
        pl.semaphore_signal(
            barrier, inc=1, device_id={"shard": lax.rem(me + off, n)}, device_id_type=MESH
        )
    for off in range(1, npop):
        pl.semaphore_signal(
            barrier, inc=1, device_id={"pop": lax.rem(mine + off, npop)}, device_id_type=MESH
        )

    def row_block(index):
        return pl.ds(pl.multiple_of(index * rows, rows), rows)

    loads[0].wait()
    for part in (0, 1):
        gathered[part, row_block(me), :] = weights_ref[0, part].astype(jnp.bfloat16)
    pl.semaphore_wait(barrier, n - 1 + npop - 1)

    half_rows, half_tokens = rows // 2, token_rows // 2

    def half_block(part, half, owner):
        start = pl.multiple_of(owner * rows + half * half_rows, half_rows)
        return gathered.at[part, pl.ds(start, half_rows), :]

    def half_of(ref, half, owner):
        return ref.at[owner, pl.ds(half * half_tokens, half_tokens), :]

    rings = [
        Halves(n, block, ring_send.at[i], ring_recv.at[i])
        for i, block in enumerate(
            [
                functools.partial(half_block, 0),
                functools.partial(half_block, 1),
                functools.partial(half_of, active_all),
                functools.partial(half_of, back_all),
            ]
        )
    ]
    down_ring, up_ring, active_ring, back_ring = rings
    group = group_of(npop, rows)
    piece = rows // group

    def piece_at(start):
        return pl.ds(pl.multiple_of(start, piece), piece)

    share = Share(
        "pop", group, lambda q: columns_in.at[:, :, piece_at(q * piece), :],
        share_send, share_recv,
    )
    sub = share.at
    columns_out = Direct(
        "shard", n,
        lambda s: columns.at[:, piece_at(s * rows + sub * piece), :],
        lambda s: columns_in.at[:, s, piece_at(sub * piece), :],
        direct_send.at[0], direct_recv.at[0],
    )
    loss_out = Direct(
        "shard", n, lambda s: loss_own, lambda s: loss_in.at[s],
        direct_send.at[1], direct_recv.at[1],
    )
    square_out = Direct(
        "shard", n, lambda s: square_own, lambda s: square_in.at[s],
        direct_send.at[2], direct_recv.at[2],
    )
    scale_out = Direct(
        "shard", n, lambda s: scale_own, lambda s: scale_in.at[s],
        direct_send.at[3], direct_recv.at[3],
    )
    pop_out = Direct(
        "pop", npop, lambda s: pop_own, lambda s: pop_in.at[s], pop_send, pop_recv
    )

    down_ring.step(0)
    up_ring.step(0)

    for load in loads[1:]:
        load.wait()
    chunk = 256
    for at in range(0, width, LANES):
        for index, source in enumerate((tokens_ref, targets_ref)):
            values = source[:, at : at + LANES].astype(jnp.float32)
            columns[index, at : at + LANES, :] = values.T.astype(jnp.bfloat16)
    columns_out.start()
    for index in range(2):
        columns_in[index, me, piece_at(sub * piece), :] = columns[
            index, piece_at(me * rows + sub * piece), :
        ]
    squares = jnp.zeros((token_rows, LANES), jnp.float32)
    for at in range(0, width, LANES):
        values = tokens_ref[:, at : at + LANES].astype(jnp.float32)
        squares += values * values
    mean = jnp.sum(squares, axis=1, keepdims=True) / width
    inverse = lax.rsqrt(mean + norm_eps)
    scale_own[...] = jnp.broadcast_to(inverse, (token_rows, LANES)).T[0:8]
    for at in range(0, width, LANES):
        values = tokens_ref[:, at : at + LANES].astype(jnp.float32)
        gain = gain_ref[:, at : at + LANES]
        normed[:, at : at + LANES] = (values * inverse * gain).astype(jnp.bfloat16)
        gain_t[at : at + LANES, :] = jnp.broadcast_to(gain, (token_rows, LANES)).T
    scale_out.start()
    scale_in[me] = scale_own[...]

    last = n // 2
    for hop in range(1, last):
        down_ring.step(hop)
        up_ring.step(hop)
        if hop == min(2, last - 1):
            columns_out.wait_recv()
            share.start()
    down_ring.step(last)

    pre = jnp.zeros((token_rows, rank), jnp.float32)
    for at in range(0, width, chunk):
        pre += jnp.dot(
            normed[:, at : at + chunk],
            gathered[0, at : at + chunk, :],
            preferred_element_type=jnp.float32,
        )
    pre = pre * down_scale
    logistic = jax.nn.sigmoid(pre)
    active = (pre * logistic).astype(jnp.bfloat16)
    active_all[me] = active
    active_ring.step(0)
    share.relay()
    slope = logistic * (1.0 + pre * (1.0 - logistic)) * up_scale
    up_ring.step(last)

    loss = jnp.zeros((1, 1), jnp.float32)
    back = jnp.zeros((token_rows, rank), jnp.float32)
    for at in range(0, width, chunk):
        held = gathered[1, at : at + chunk, :]
        branch = lax.dot_general(
            active, held, (((1,), (1,)), ((), ())), preferred_element_type=jnp.float32
        )
        residual = (
            tokens_ref[:, at : at + chunk].astype(jnp.float32)
            + branch * up_scale
            - targets_ref[:, at : at + chunk].astype(jnp.float32)
        )
        loss += total_of(residual * residual)
        double = 2.0 * residual
        back += jnp.dot(double.astype(jnp.bfloat16), held, preferred_element_type=jnp.float32)
    back_all[me] = (back * slope).astype(jnp.bfloat16)
    loss_own[...] = jnp.broadcast_to(loss, loss_own.shape)
    back_ring.step(0)
    active_ring.step(1)
    loss_out.start()
    loss_in[me] = loss_own[...]
    share.wait_recv()
    scale_out.wait_recv()

    def add_block(owner, first):
        used = active_all[owner]
        branch = lax.dot_general(
            gathered[1, row_block(me), :], used, (((1,), (1,)), ((), ())),
            preferred_element_type=jnp.float32,
        )
        residual = (
            columns_in[0, owner].astype(jnp.float32)
            + branch * up_scale
            - columns_in[1, owner].astype(jnp.float32)
        )
        upstream = (2.0 * residual).astype(jnp.bfloat16)
        scaled = columns_in[0, owner].astype(jnp.float32) * scale_in[owner][0:1, :]
        scaled = (scaled * gain_t[row_block(me), :]).astype(jnp.bfloat16)
        down = jnp.dot(scaled, back_all[owner], preferred_element_type=jnp.float32)
        up = jnp.dot(upstream, used, preferred_element_type=jnp.float32)
        if first:
            grad_ref[0], grad_ref[1] = down, up
        else:
            grad_ref[0] += down
            grad_ref[1] += up

    add_block(me, True)
    for hop in range(1, last + 1):
        back_ring.step(hop)
        if hop > 1:
            active_ring.step(hop)
        add_block(back_ring.shard(back_ring.pos - hop), False)
        if hop < n - hop:
            add_block(back_ring.shard(back_ring.pos + hop), False)

    sums = []
    for part in (0, 1):
        acc = grad_ref[part] * (down_scale, up_scale)[part]
        grad_ref[part] = acc
        sums.append(total_of(acc * acc))
    line = lax.broadcasted_iota(jnp.int32, square_own.shape, 0)
    square_own[...] = jnp.where(
        line == 0,
        jnp.broadcast_to(sums[0], square_own.shape),
        jnp.broadcast_to(sums[1], square_own.shape),
    )
    square_out.start()
    square_in[me] = square_own[...]
    loss_out.wait_recv()
    losses = loss_in[0]
    for j in range(1, n):
        losses += loss_in[j]
    pop_own[...] = losses
    pop_out.start()
    pop_in[mine] = losses
    square_out.wait_recv()
    both = square_in[0]
    for j in range(1, n):
        both += square_in[j]
    stats_ref[...] = both
    pop_out.wait_recv()
    losses_ref[...] = pop_in[...]
    for item in (*rings, columns_out, share, scale_out, loss_out, square_out, pop_out):
        item.drain()


def exchange(mesh_shape, tokens, targets, gain, weights):
    n, npop = mesh_shape["shard"], mesh_shape["pop"]
    token_rows, width = tokens.shape
    rank = weights.shape[-1]
    rows = width // n
    wide, narrow = jnp.float32, jnp.bfloat16
    tile = (8, LANES)
    vmem = pl.BlockSpec(memory_space=pltpu.VMEM)
    anywhere = pl.BlockSpec(memory_space=pl.ANY)
    return pl.pallas_call(
        functools.partial(exchange_kernel, n, npop),
        out_shape=(
            jax.ShapeDtypeStruct((2, rows, rank), wide),
            jax.ShapeDtypeStruct(tile, wide),
            jax.ShapeDtypeStruct((npop, *tile), wide),
        ),
        in_specs=[anywhere] * 4,
        out_specs=(vmem, vmem, vmem),
        scratch_shapes=[
            pltpu.VMEM(tokens.shape, tokens.dtype),
            pltpu.VMEM(targets.shape, targets.dtype),
            pltpu.VMEM(gain.shape, gain.dtype),
            pltpu.VMEM(weights.shape, weights.dtype),
            pltpu.SemaphoreType.DMA((4,)),
            pltpu.VMEM((2, width, rank), narrow),
            pltpu.VMEM((token_rows, width), narrow),
            pltpu.VMEM((2, width, token_rows), narrow),
            pltpu.VMEM((2, n, rows, token_rows), narrow),
            pltpu.VMEM((width, token_rows), wide),
            pltpu.VMEM((8, token_rows), wide),
            pltpu.VMEM((n, 8, token_rows), wide),
            pltpu.VMEM((n, token_rows, rank), narrow),
            pltpu.VMEM((n, token_rows, rank), narrow),
            pltpu.VMEM(tile, wide),
            pltpu.VMEM((n, *tile), wide),
            pltpu.VMEM(tile, wide),
            pltpu.VMEM((n, *tile), wide),
            pltpu.VMEM(tile, wide),
            pltpu.VMEM((npop, *tile), wide),
            pltpu.SemaphoreType.DMA((4, 2, n + 2)),
            pltpu.SemaphoreType.DMA((4, 2, n + 2)),
            pltpu.SemaphoreType.DMA((4, n)),
            pltpu.SemaphoreType.DMA((4, n)),
            pltpu.SemaphoreType.DMA((npop,)),
            pltpu.SemaphoreType.DMA((npop,)),
            pltpu.SemaphoreType.DMA((4,)),
            pltpu.SemaphoreType.DMA((4,)),
        ],
        compiler_params=pltpu.CompilerParams(
            collective_id=0, has_side_effects=True
        ),
        name="exchange",
    )(tokens, targets, gain, weights)


def update_kernel(
    npop, count, loss_count, base_ref, shift_ref, stats_ref, losses_ref, perturbation_ref,
    accumulated_ref, grad_ref, weights_ref, first_ref, second_ref,
    weights_out, first_out, second_out, unroll_out, outer_out, learned_ref,
):
    part = pl.program_id(0)
    mine = lax.axis_index("pop")
    units = base_ref.shape[0] // 6
    height = grad_ref.shape[1]
    block = min(32, height)

    @pl.when((part == 0) & (pl.program_id(1) == 0))
    def _():
        polarity = (1 - 2 * lax.rem(mine, 2)).astype(jnp.float32)
        pair = mine // 2

        def blend(at, carry):
            learned_ref[at] = base_ref[at] + polarity * shift_ref[pair, at]
            return carry

        lax.fori_loop(0, 6 * units, blend, 0, unroll=16)
        unroll_out[...] = losses_ref[mine][0:1, 0:1] / loss_count
        outer = jnp.zeros(outer_out.shape, jnp.float32)
        for q in range(npop // 2):
            differ = (losses_ref[2 * q] - losses_ref[2 * q + 1])[0:1, 0:1] / loss_count
            outer += differ * (accumulated_ref[q : q + 1, :] + perturbation_ref[q : q + 1, :])
        outer_out[...] = outer / (2 * (npop // 2))

    square = jnp.where(part == 0, stats_ref[0:1, 0:1], stats_ref[1:2, 0:1])
    scale = lax.rsqrt(square / count + grad_eps)

    @pl.loop(0, height // block)
    def _(at):
        here = pl.ds(pl.multiple_of(at * block, block), block)
        scaled = grad_ref[0, here, :] * scale
        first = beta_one * first_ref[0, 0, here, :] + (1.0 - beta_one) * scaled
        second = beta_two * second_ref[0, 0, here, :] + (1.0 - beta_two) * scaled * scaled
        first_out[0, 0, here, :] = first
        second_out[0, 0, here, :] = second
        inverse = lax.rsqrt(second)
        slope = scaled * inverse
        momentum = first * inverse
        held = weights_ref[0, 0, here, :]
        shift = momentum
        gate = jnp.zeros_like(momentum)
        for unit in range(units):
            hidden = jnp.tanh(
                slope * learned_ref[unit]
                + momentum * learned_ref[units + unit]
                + (held * learned_ref[2 * units + unit] + learned_ref[3 * units + unit])
            )
            shift = shift + hidden * learned_ref[4 * units + unit]
            gate = gate + hidden * learned_ref[5 * units + unit]
        weights_out[0, 0, here, :] = held - step_size * shift * jnp.exp(jnp.tanh(gate))


def update(base, perturbation, accumulated, stats, losses, grad, weights, first, second, npop,
           count, loss_count):
    _, _, rows, rank = weights.shape
    height = min(rows, 128)
    spec = pl.BlockSpec((1, 1, height, rank), lambda p, i: (0, p, i, 0))
    shape = jax.ShapeDtypeStruct(weights.shape, jnp.float32)
    scalars = pl.BlockSpec(memory_space=pltpu.SMEM)

    def whole(extent):
        return pl.BlockSpec(extent, lambda p, i: (0,) * len(extent))

    outer_shape = (1, base.shape[0])
    return pl.pallas_call(
        functools.partial(update_kernel, npop, count, loss_count),
        grid=(2, rows // height),
        out_shape=(
            shape,
            shape,
            shape,
            jax.ShapeDtypeStruct((1, 1), jnp.float32),
            jax.ShapeDtypeStruct(outer_shape, jnp.float32),
        ),
        in_specs=[
            scalars,
            scalars,
            whole(stats.shape),
            whole(losses.shape),
            whole(perturbation.shape),
            whole(accumulated.shape),
            pl.BlockSpec((1, height, rank), lambda p, i: (p, i, 0)),
            spec,
            spec,
            spec,
        ],
        out_specs=(spec, spec, spec, whole((1, 1)), whole(outer_shape)),
        scratch_shapes=[pltpu.SMEM(base.shape, jnp.float32)],
        name="update",
    )(base, perturbation, stats, losses, perturbation, accumulated, grad, weights, first, second)


def local(
    mesh_shape,
    tokens,
    targets,
    norm_gain,
    weights,
    first_moment,
    second_moment,
    learned_params,
    perturbation,
    accumulated,
):
    n, npop = mesh_shape["shard"], mesh_shape["pop"]
    token_rows, width = tokens.shape
    rank = weights.shape[-1]
    grad, stats, losses = exchange(mesh_shape, tokens, targets, norm_gain[None], weights)
    new_weights, new_first, new_second, unroll, outer = update(
        learned_params, perturbation, accumulated, stats, losses, grad, weights, first_moment,
        second_moment, npop, width * rank, token_rows * n * width,
    )
    return (new_weights, new_first, new_second, unroll[0], outer[0])


def solution(mesh):
    rows = P("pop", None, "shard", None)
    return jax.shard_map(
        functools.partial(local, dict(mesh.shape)),
        mesh=mesh,
        in_specs=(P("shard", None), P("shard", None), P(), rows, rows, rows, P(), P(), P()),
        out_specs=(rows, rows, rows, P("pop"), P()),
        check_vma=False,
    )
```
